32 devices in a mesh: ctx: 8 (over y, x, core), shard: 4 (over z).
Axes of the slice: x: 2, y: 2, z: 4, core: 2. Of those that a mesh axis runs over, the one named last changes fastest.
Arguments:
- tokens: bfloat16 [4096, 640], P(('ctx', 'shard')), may hold values from -36 to 36
- positions: int32 [4096], replicated, may hold values from 0 to 4095, as said below
- cotangent: bfloat16 [4096, 640], P(('ctx', 'shard')), may hold values from -6 to 6
- query_weight: float32 [640, 1024], P('ctx', 'shard'), may hold values from -0.25 to 0.25
- query_first: float32 [640, 1024], P('ctx', 'shard'), may hold values from -112 to 112
- query_second: float32 [640, 1024], P('ctx', 'shard'), may hold values from 40.96 to 4096
- keyval_weight: float32 [2, 640, 256], P(None, 'ctx', 'shard'), may hold values from -0.25 to 0.25
- keyval_first: float32 [2, 640, 256], P(None, 'ctx', 'shard'), may hold values from -112 to 112
- keyval_second: float32 [2, 640, 256], P(None, 'ctx', 'shard'), may hold values from 40.96 to 4096
- output_weight: float32 [1024, 640], P('shard', 'ctx'), may hold values from -0.1875 to 0.1875
- output_first: float32 [1024, 640], P('shard', 'ctx'), may hold values from -112 to 112
- output_second: float32 [1024, 640], P('shard', 'ctx'), may hold values from 40.96 to 4096
- gateup_weight: float32 [2, 640, 2048], P(None, 'ctx', 'shard'), may hold values from -0.25 to 0.25
- gateup_first: float32 [2, 640, 2048], P(None, 'ctx', 'shard'), may hold values from -112 to 112
- gateup_second: float32 [2, 640, 2048], P(None, 'ctx', 'shard'), may hold values from 40.96 to 4096
- down_weight: float32 [2048, 640], P('shard', 'ctx'), may hold values from -0.125 to 0.125
- down_first: float32 [2048, 640], P('shard', 'ctx'), may hold values from -112 to 112
- down_second: float32 [2048, 640], P('shard', 'ctx'), may hold values from 40.96 to 4096
- norm_scales: float32 [4, 640], replicated, may hold values from -0.3 to 0.3
- norm_first: float32 [4, 640], replicated, may hold values from -112 to 112
- norm_second: float32 [4, 640], replicated, may hold values from 40.96 to 4096
- head_scales: float32 [2, 256], replicated, may hold values from -0.3 to 0.3
- head_first: float32 [2, 256], replicated, may hold values from -112 to 112
- head_second: float32 [2, 256], replicated, may hold values from 40.96 to 4096
Outputs:
- block_out: bfloat16 [4096, 640], P(('ctx', 'shard'))
- tokens_grad: bfloat16 [4096, 640], P(('ctx', 'shard'))
- query_grad: float32 [640, 1024], P('ctx', 'shard')
- query_new: float32 [640, 1024], P('ctx', 'shard')
- query_first_new: float32 [640, 1024], P('ctx', 'shard')
- query_second_new: float32 [640, 1024], P('ctx', 'shard')
- keyval_grad: float32 [2, 640, 256], P(None, 'ctx', 'shard')
- keyval_new: float32 [2, 640, 256], P(None, 'ctx', 'shard')
- keyval_first_new: float32 [2, 640, 256], P(None, 'ctx', 'shard')
- keyval_second_new: float32 [2, 640, 256], P(None, 'ctx', 'shard')
- output_grad: float32 [1024, 640], P('shard', 'ctx')
- output_new: float32 [1024, 640], P('shard', 'ctx')
- output_first_new: float32 [1024, 640], P('shard', 'ctx')
- output_second_new: float32 [1024, 640], P('shard', 'ctx')
- gateup_grad: float32 [2, 640, 2048], P(None, 'ctx', 'shard')
- gateup_new: float32 [2, 640, 2048], P(None, 'ctx', 'shard')
- gateup_first_new: float32 [2, 640, 2048], P(None, 'ctx', 'shard')
- gateup_second_new: float32 [2, 640, 2048], P(None, 'ctx', 'shard')
- down_grad: float32 [2048, 640], P('shard', 'ctx')
- down_new: float32 [2048, 640], P('shard', 'ctx')
- down_first_new: float32 [2048, 640], P('shard', 'ctx')
- down_second_new: float32 [2048, 640], P('shard', 'ctx')
- norm_grad: float32 [4, 640], replicated
- norm_new: float32 [4, 640], replicated
- norm_first_new: float32 [4, 640], replicated
- norm_second_new: float32 [4, 640], replicated
- head_grad: float32 [2, 256], replicated
- head_new: float32 [2, 256], replicated
- head_first_new: float32 [2, 256], replicated
- head_second_new: float32 [2, 256], replicated
The draws below stay inside these ranges and needn't reach their ends.
Inputs may be any that keep to these rules, and one draw needn't show every extreme that they name: A permutation of the 4096 positions in mirrored pairs of blocks of 256: the device at ctx index c and shard index s holds in its first 64 rows the positions b * 256 + s * 64 + r, r counting up, of one block b below 8, and in its other rows the same offsets in block 15 - b; every ctx index has its own b.
All inputs are finite; a program needn't handle non-finite values.
Results may differ from the reference program's by a relative error of at most 0.023.
Values may be sent and summed in bfloat16 or wider, within the bound.
No kernel may reach another device: no remote copies, remote signals or barrier semaphores. Data moves between devices by JAX's collectives and lax.ppermute only.
A program may use at most 256 MiB of HBM per device.

```python
import math
import jax
import jax.numpy as jnp
from jax import lax

D = 640
HEADS = 4
HEAD = 256
FF = 2048
TOK_DEV = 128
STEP = 3
PAIRS = 8
BLOCK = 256
SEQ = 4096


def draw_positions(key, part):
    shard_count = 2 * BLOCK // TOK_DEV
    order = jax.random.permutation(key, PAIRS).astype(jnp.int32)
    index = jnp.arange(SEQ, dtype=jnp.int32)
    device = index // TOK_DEV
    row_in = index % TOK_DEV
    ctx_of = device // shard_count
    shard_of = device % shard_count
    half_len = TOK_DEV // 2
    chosen = order[ctx_of]
    block_of = jnp.where(row_in < half_len, chosen, 2 * PAIRS - 1 - chosen)
    return (block_of * BLOCK + shard_of * half_len + row_in % half_len).astype(jnp.int32)


def draw_head_scales(key, part):
    return jax.random.uniform(key, (2, HEAD), jnp.float32, -0.3, 0.3)


def draw_tokens(key, part):
    first_key, col_key, row_key = jax.random.split(key, 3)
    columns = jnp.exp(jax.random.uniform(col_key, (1, D), jnp.float32, math.log(0.3), math.log(3.0)))
    rows_scale = jnp.exp(jax.random.uniform(row_key, (SEQ, 1), jnp.float32, math.log(0.3), math.log(3.0)))
    base = jax.random.normal(first_key, (SEQ, D), jnp.float32)
    base = jnp.clip(base, -4.0, 4.0)
    return (base * columns * rows_scale).astype(jnp.bfloat16)


def levels(stream_key, dims, cuts, smallest, high):
    loudness = 1.0
    for position, parts in cuts:
        steps = jax.random.uniform(jax.random.fold_in(jax.random.fold_in(stream_key, 6), position), (parts,), jnp.float32, smallest / len(cuts), high / len(cuts))
        loudness = loudness * jnp.repeat(jnp.exp(steps), dims[position] // parts).reshape((-1,) + (1,) * (len(dims) - 1 - position))
    return loudness


def noise(key, extent, deviation, bound, pieces=(), held_as=jnp.bfloat16):
    level = levels(key, extent, pieces, -0.22, 0.18) if pieces else 1.0
    array = jax.random.normal(key, extent, jnp.float32) * deviation * level
    return jnp.minimum(jnp.maximum(array, -bound), bound).astype(held_as)


def setup_inputs(seed: int = 0) -> dict:
    key_of = jax.random.split(jax.random.key(seed), 25)
    return {
        "tokens": draw_tokens(jax.random.fold_in(key_of[24], 71), 0),
        "positions": draw_positions(jax.random.fold_in(key_of[24], 71), 0),
        "cotangent": noise(key_of[2], (SEQ, D), 1.0, 6.0, ((0, 32),)),
        "query_weight": noise(key_of[3], (D, HEADS * HEAD), D ** -0.5, 0.25, ((0, 8), (1, 4)), jnp.float32),
        "query_first": noise(key_of[4], (D, HEADS * HEAD), (0.3 * SEQ ** 0.5), 112.0, ((0, 8), (1, 4)), jnp.float32),
        "query_second": jnp.clip(jnp.exp(math.log(4096.0) - 4.6051702 * jax.random.uniform(key_of[5], (D, HEADS * HEAD), jnp.float32) ** levels(key_of[5], (D, HEADS * HEAD), ((0, 8), (1, 4)), -0.2, 0.2)), 40.96, 4096.0),
        "keyval_weight": noise(key_of[6], (2, D, HEAD), D ** -0.5, 0.25, ((1, 8), (2, 4)), jnp.float32),
        "keyval_first": noise(key_of[7], (2, D, HEAD), (0.3 * SEQ ** 0.5), 112.0, ((1, 8), (2, 4)), jnp.float32),
        "keyval_second": jnp.clip(jnp.exp(math.log(4096.0) - 4.6051702 * jax.random.uniform(key_of[8], (2, D, HEAD), jnp.float32) ** levels(key_of[8], (2, D, HEAD), ((1, 8), (2, 4)), -0.2, 0.2)), 40.96, 4096.0),
        "output_weight": noise(key_of[9], (HEADS * HEAD, D), (HEADS * HEAD) ** -0.5, 0.1875, ((0, 4), (1, 8)), jnp.float32),
        "output_first": noise(key_of[10], (HEADS * HEAD, D), (0.3 * SEQ ** 0.5), 112.0, ((0, 4), (1, 8)), jnp.float32),
        "output_second": jnp.clip(jnp.exp(math.log(4096.0) - 4.6051702 * jax.random.uniform(key_of[11], (HEADS * HEAD, D), jnp.float32) ** levels(key_of[11], (HEADS * HEAD, D), ((0, 4), (1, 8)), -0.2, 0.2)), 40.96, 4096.0),
        "gateup_weight": noise(key_of[12], (2, D, FF), D ** -0.5, 0.25, ((1, 8), (2, 4)), jnp.float32),
        "gateup_first": noise(key_of[13], (2, D, FF), (0.3 * SEQ ** 0.5), 112.0, ((1, 8), (2, 4)), jnp.float32),
        "gateup_second": jnp.clip(jnp.exp(math.log(4096.0) - 4.6051702 * jax.random.uniform(key_of[14], (2, D, FF), jnp.float32) ** levels(key_of[14], (2, D, FF), ((1, 8), (2, 4)), -0.2, 0.2)), 40.96, 4096.0),
        "down_weight": noise(key_of[15], (FF, D), FF ** -0.5, 0.125, ((0, 4), (1, 8)), jnp.float32),
        "down_first": noise(key_of[16], (FF, D), (0.3 * SEQ ** 0.5), 112.0, ((0, 4), (1, 8)), jnp.float32),
        "down_second": jnp.clip(jnp.exp(math.log(4096.0) - 4.6051702 * jax.random.uniform(key_of[17], (FF, D), jnp.float32) ** levels(key_of[17], (FF, D), ((0, 4), (1, 8)), -0.2, 0.2)), 40.96, 4096.0),
        "norm_scales": jnp.clip(jax.random.uniform(key_of[18], (4, D), jnp.float32, -0.3, 0.3), -0.3, 0.3),
        "norm_first": noise(key_of[19], (4, D), (0.3 * SEQ ** 0.5), 112.0, (), jnp.float32),
        "norm_second": jnp.clip(jnp.exp(jax.random.uniform(key_of[20], (4, D), jnp.float32, math.log(40.96), math.log(4096.0))), 40.96, 4096.0),
        "head_scales": draw_head_scales(jax.random.fold_in(key_of[24], 71), 0),
        "head_first": noise(key_of[22], (2, HEAD), (0.3 * SEQ ** 0.5), 112.0, (), jnp.float32),
        "head_second": jnp.clip(jnp.exp(jax.random.uniform(key_of[23], (2, HEAD), jnp.float32, math.log(40.96), math.log(4096.0))), 40.96, 4096.0),
    }


norm_eps = 1e-06
rope_base = 1000000.0
score_scale = 0.0625
learn_rate = 0.02
beta_first = 0.9
beta_second = 0.95
adam_eps = 1e-08
weight_decay = 0.1
gelu_coef = 0.7978845608028654
masked_value = -1e+30

def rms_forward(values):
    inverse = lax.rsqrt(lax.optimization_barrier(jnp.mean(values * values, axis=-1, keepdims=True)) + norm_eps)
    return (values * inverse, inverse)

def rms_backward(normed, inverse, upstream):
    return inverse * (upstream - normed * lax.optimization_barrier(jnp.mean(upstream * normed, axis=-1, keepdims=True)))

def rotate(values):
    middle = values.shape[-1] // 2
    return jnp.concatenate([-values[..., middle:], values[..., :middle]], axis=-1)

def rotate_back(values):
    middle = values.shape[-1] // 2
    return jnp.concatenate([values[..., middle:], -values[..., :middle]], axis=-1)

def rope_tables(places):
    middle = HEAD // 2
    freqs = rope_base ** (-(jnp.arange(middle, dtype=jnp.float32) * 2.0 / HEAD))
    angles = places.astype(jnp.float32)[:, None] * freqs[None, :]
    cosine = jnp.cos(angles)
    sine = jnp.sin(angles)
    return (jnp.concatenate([cosine, cosine], axis=-1), jnp.concatenate([sine, sine], axis=-1))

def gelu_parts(values):
    inner = gelu_coef * (values + 0.044715 * values * values * values)
    tangent = jnp.tanh(inner)
    result = 0.5 * values * (1.0 + tangent)
    slope = 0.5 * (1.0 + tangent) + 0.5 * values * (1.0 - tangent * tangent) * gelu_coef * (1.0 + 3.0 * 0.044715 * values * values)
    return (result, slope)

def adam_update(weight, first, second, grad):
    first_new = beta_first * first + (1.0 - beta_first) * grad
    second_new = beta_second * second + (1.0 - beta_second) * grad * grad
    first_hat = first_new / (1.0 - beta_first ** STEP)
    second_hat = second_new / (1.0 - beta_second ** STEP)
    weight_new = weight - learn_rate * (first_hat / (jnp.sqrt(second_hat) + adam_eps) + weight_decay * weight)
    return (grad, weight_new, first_new, second_new)

def reference(tokens, positions, cotangent, query_weight, query_first, query_second, keyval_weight, keyval_first, keyval_second, output_weight, output_first, output_second, gateup_weight, gateup_first, gateup_second, down_weight, down_first, down_second, norm_scales, norm_first, norm_second, head_scales, head_first, head_second):
    bfloat = jnp.bfloat16
    single = jnp.float32
    query_full = query_weight.astype(bfloat)
    keyval_full = keyval_weight.astype(bfloat)
    output_full = output_weight.astype(bfloat)
    gateup_full = gateup_weight.astype(bfloat)
    down_full = down_weight.astype(bfloat)
    inputs = tokens.astype(single)
    normed_in, inverse_in = rms_forward(inputs)
    attn_in = (normed_in * (1.0 + norm_scales[0])).astype(bfloat)
    query_proj = jnp.dot(attn_in, query_full, preferred_element_type=single)
    key_proj = jnp.dot(attn_in, keyval_full[0], preferred_element_type=single)
    value_proj = jnp.dot(attn_in, keyval_full[1], preferred_element_type=single)
    cosine, sine = rope_tables(positions)
    query_normed, query_inverse = rms_forward(query_proj.reshape(SEQ, HEADS, HEAD))
    query_scaled = query_normed * (1.0 + head_scales[0])
    query_rot = query_scaled * cosine[:, None, :] + rotate(query_scaled) * sine[:, None, :]
    query_rows = query_rot.astype(bfloat).reshape(SEQ * HEADS, HEAD)
    key_normed, key_inverse = rms_forward(key_proj)
    key_scaled = key_normed * (1.0 + head_scales[1])
    keys_all = (key_scaled * cosine + rotate(key_scaled) * sine).astype(bfloat)
    values_all = value_proj.astype(bfloat)
    row_at = jnp.repeat(positions, HEADS)
    block_len = min(1024, SEQ)
    block_count = SEQ // block_len
    query_blocks = query_rows.reshape(block_count, block_len * HEADS, HEAD)
    at_blocks = row_at.reshape(block_count, block_len * HEADS)

    def forward_block(block_inputs):
        rows_here, at_here = block_inputs
        scores = jnp.dot(rows_here, keys_all.T, preferred_element_type=single) * score_scale
        visible = positions[None, :] <= at_here[:, None]
        scores = jnp.where(visible, scores, masked_value)
        peak_row = lax.optimization_barrier(jnp.max(scores, axis=-1, keepdims=True))
        total_row = lax.optimization_barrier(jnp.sum(jnp.where(visible, jnp.exp(scores - peak_row), 0.0), axis=-1, keepdims=True))
        log_total = peak_row + jnp.log(total_row)
        weights = jnp.where(visible, jnp.exp(scores - log_total), 0.0)
        mixed = jnp.dot(weights.astype(bfloat), values_all, preferred_element_type=single)
        return (mixed, log_total)
    attn_blocks, log_blocks = lax.map(forward_block, (query_blocks, at_blocks))
    attn_rows = attn_blocks.reshape(SEQ * HEADS, HEAD)
    attn_b = attn_rows.reshape(SEQ, HEADS * HEAD).astype(bfloat)
    attn_out = jnp.dot(attn_b, output_full, preferred_element_type=single)
    out_normed, out_inverse = rms_forward(attn_out)
    hidden_in = inputs + out_normed * (1.0 + norm_scales[1])
    mid_normed, mid_inverse = rms_forward(hidden_in)
    ffn_in = (mid_normed * (1.0 + norm_scales[2])).astype(bfloat)
    gate_pre = jnp.dot(ffn_in, gateup_full[0], preferred_element_type=single)
    up_pre = jnp.dot(ffn_in, gateup_full[1], preferred_element_type=single)
    gate_value, gate_slope = gelu_parts(gate_pre)
    hidden_b = (gate_value * up_pre).astype(bfloat)
    ffn_out = jnp.dot(hidden_b, down_full, preferred_element_type=single)
    ffn_normed, ffn_inverse = rms_forward(ffn_out)
    block_out = (hidden_in + ffn_normed * (1.0 + norm_scales[3])).astype(bfloat)
    upstream = cotangent.astype(single)
    grad_norm3 = lax.optimization_barrier(jnp.sum(upstream * ffn_normed, axis=0))
    ffn_grad = rms_backward(ffn_normed, ffn_inverse, upstream * (1.0 + norm_scales[3])).astype(bfloat)
    down_wgrad = jnp.dot(hidden_b.T, ffn_grad, preferred_element_type=single)
    hidden_grad = jnp.dot(ffn_grad, down_full.T, preferred_element_type=single)
    gate_grad = (hidden_grad * up_pre * gate_slope).astype(bfloat)
    up_grad = (hidden_grad * gate_value).astype(bfloat)
    gateup_wgrad = jnp.stack([jnp.dot(ffn_in.T, gate_grad, preferred_element_type=single), jnp.dot(ffn_in.T, up_grad, preferred_element_type=single)])
    ffn_in_grad = jnp.dot(gate_grad, gateup_full[0].T, preferred_element_type=single) + jnp.dot(up_grad, gateup_full[1].T, preferred_element_type=single)
    grad_norm2 = lax.optimization_barrier(jnp.sum(ffn_in_grad * mid_normed, axis=0))
    residual_grad = upstream + rms_backward(mid_normed, mid_inverse, ffn_in_grad * (1.0 + norm_scales[2]))
    grad_norm1 = lax.optimization_barrier(jnp.sum(residual_grad * out_normed, axis=0))
    attn_out_grad = rms_backward(out_normed, out_inverse, residual_grad * (1.0 + norm_scales[1])).astype(bfloat)
    output_wgrad = jnp.dot(attn_b.T, attn_out_grad, preferred_element_type=single)
    attn_grad_b = jnp.dot(attn_out_grad, output_full.T, preferred_element_type=single).astype(bfloat)
    grad_rows = attn_grad_b.reshape(SEQ * HEADS, HEAD)
    row_delta = lax.optimization_barrier(jnp.sum(grad_rows.astype(single) * attn_rows, axis=-1, keepdims=True))

    def backward_block(carry, block_inputs):
        key_acc, value_acc = carry
        rows_here, at_here, log_here, grad_here, delta_here = block_inputs
        scores = jnp.dot(rows_here, keys_all.T, preferred_element_type=single) * score_scale
        visible = positions[None, :] <= at_here[:, None]
        scores = jnp.where(visible, scores, masked_value)
        weights = jnp.where(visible, jnp.exp(scores - log_here), 0.0)
        grad_weights = jnp.dot(grad_here, values_all.T, preferred_element_type=single)
        grad_scores = (weights * (grad_weights - delta_here)).astype(bfloat)
        query_part = jnp.dot(grad_scores, keys_all, preferred_element_type=single) * score_scale
        key_acc = key_acc + jnp.dot(grad_scores.T, rows_here, preferred_element_type=single) * score_scale
        value_acc = value_acc + jnp.dot(weights.astype(bfloat).T, grad_here, preferred_element_type=single)
        return ((key_acc, value_acc), query_part)
    zero_keys = jnp.zeros((SEQ, HEAD), single)
    (key_rot_grad, value_grad), query_parts = lax.scan(backward_block, (zero_keys, zero_keys), (query_blocks, at_blocks, log_blocks, grad_rows.reshape(block_count, block_len * HEADS, HEAD), row_delta.reshape(block_count, block_len * HEADS, 1)))
    query_rot_grad = query_parts.reshape(SEQ, HEADS, HEAD)
    query_rope_grad = query_rot_grad * cosine[:, None, :] + rotate_back(query_rot_grad * sine[:, None, :])
    grad_head0 = lax.optimization_barrier(jnp.sum(query_rope_grad * query_normed, axis=(0, 1)))
    query_proj_grad = rms_backward(query_normed, query_inverse, query_rope_grad * (1.0 + head_scales[0])).reshape(SEQ, HEADS * HEAD).astype(bfloat)
    key_rope_grad = key_rot_grad * cosine + rotate_back(key_rot_grad * sine)
    grad_head1 = lax.optimization_barrier(jnp.sum(key_rope_grad * key_normed, axis=0))
    key_proj_grad = rms_backward(key_normed, key_inverse, key_rope_grad * (1.0 + head_scales[1])).astype(bfloat)
    value_proj_grad = value_grad.astype(bfloat)
    query_wgrad = jnp.dot(attn_in.T, query_proj_grad, preferred_element_type=single)
    keyval_wgrad = jnp.stack([jnp.dot(attn_in.T, key_proj_grad, preferred_element_type=single), jnp.dot(attn_in.T, value_proj_grad, preferred_element_type=single)])
    attn_in_grad = jnp.dot(query_proj_grad, query_full.T, preferred_element_type=single) + jnp.dot(key_proj_grad, keyval_full[0].T, preferred_element_type=single) + jnp.dot(value_proj_grad, keyval_full[1].T, preferred_element_type=single)
    grad_norm0 = lax.optimization_barrier(jnp.sum(attn_in_grad * normed_in, axis=0))
    tokens_grad = (residual_grad + rms_backward(normed_in, inverse_in, attn_in_grad * (1.0 + norm_scales[0]))).astype(bfloat)
    norm_wgrad = jnp.stack([grad_norm0, grad_norm1, grad_norm2, grad_norm3])
    head_wgrad = jnp.stack([grad_head0, grad_head1])
    query_set = adam_update(query_weight, query_first, query_second, query_wgrad)
    keyval_set = adam_update(keyval_weight, keyval_first, keyval_second, keyval_wgrad)
    output_set = adam_update(output_weight, output_first, output_second, output_wgrad)
    gateup_set = adam_update(gateup_weight, gateup_first, gateup_second, gateup_wgrad)
    down_set = adam_update(down_weight, down_first, down_second, down_wgrad)
    norm_set = adam_update(norm_scales, norm_first, norm_second, norm_wgrad)
    head_set = adam_update(head_scales, head_first, head_second, head_wgrad)
    return (block_out, tokens_grad, query_set[0], query_set[1], query_set[2], query_set[3], keyval_set[0], keyval_set[1], keyval_set[2], keyval_set[3], output_set[0], output_set[1], output_set[2], output_set[3], gateup_set[0], gateup_set[1], gateup_set[2], gateup_set[3], down_set[0], down_set[1], down_set[2], down_set[3], norm_set[0], norm_set[1], norm_set[2], norm_set[3], head_set[0], head_set[1], head_set[2], head_set[3])
```

```python
import jax
import jax.numpy as jnp
from jax import lax
from jax.experimental import pallas as pl
from jax.experimental.pallas import tpu as pltpu
from jax.sharding import PartitionSpec as P

HEADS = 4
HEAD = 256
STEP = 3


norm_eps = 1e-06
rope_base = 1000000.0
score_scale = 0.0625
learn_rate = 0.02
beta_first = 0.9
beta_second = 0.95
adam_eps = 1e-08
weight_decay = 0.1
gelu_coef = 0.7978845608028654
masked_value = -1e30


def rms_forward(values):
    inverse = lax.rsqrt(jnp.mean(values * values, axis=-1, keepdims=True) + norm_eps)
    return (values * inverse, inverse)


def rms_backward(normed, inverse, upstream):
    return inverse * (upstream - normed * jnp.mean(upstream * normed, axis=-1, keepdims=True))


def rotate(values):
    middle = values.shape[-1] // 2
    return jnp.concatenate([-values[..., middle:], values[..., :middle]], axis=-1)


def rotate_back(values):
    middle = values.shape[-1] // 2
    return jnp.concatenate([values[..., middle:], -values[..., :middle]], axis=-1)


def rope_tables(places):
    middle = HEAD // 2
    freqs = rope_base ** (-(jnp.arange(middle, dtype=jnp.float32) * 2.0 / HEAD))
    angles = places.astype(jnp.float32)[:, None] * freqs[None, :]
    cosine = jnp.cos(angles)
    sine = jnp.sin(angles)
    return (jnp.concatenate([cosine, cosine], axis=-1), jnp.concatenate([sine, sine], axis=-1))


def gelu_parts(values):
    inner = gelu_coef * (values + 0.044715 * values * values * values)
    tangent = jnp.tanh(inner)
    result = 0.5 * values * (1.0 + tangent)
    slope = 0.5 * (1.0 + tangent) + 0.5 * values * (1.0 - tangent * tangent) * gelu_coef * (
        1.0 + 3.0 * 0.044715 * values * values
    )
    return (result, slope)


def adam_update(weight, first, second, grad):
    first_new = beta_first * first + (1.0 - beta_first) * grad
    second_new = beta_second * second + (1.0 - beta_second) * grad * grad
    first_hat = first_new / (1.0 - beta_first**STEP)
    second_hat = second_new / (1.0 - beta_second**STEP)
    weight_new = weight - learn_rate * (
        first_hat / (jnp.sqrt(second_hat) + adam_eps) + weight_decay * weight
    )
    return (grad, weight_new, first_new, second_new)


def swap(piece, axis, distance):
    return lax.ppermute(piece, axis, [(i, i ^ distance) for i in range(lax.axis_size(axis))])


def chip_count():
    return lax.axis_size("ctx") // 2


def gather_shard(piece, dim):
    return jnp.concatenate(
        [piece] + [swap(piece, "shard", j) for j in range(1, lax.axis_size("shard"))], axis=dim
    )


def gather_chips(piece, dim):
    return jnp.concatenate(
        [piece] + [swap(piece, "ctx", 2 * k) for k in range(1, chip_count())], axis=dim
    )


def gather_cores(piece, dim):
    return jnp.concatenate([piece, swap(piece, "ctx", 1)], axis=dim)


def tree_sum(terms):
    while len(terms) > 1:
        terms = [terms[i] + terms[i + 1] for i in range(0, len(terms), 2)]
    return terms[0]


def scatter_cores(terms, dim):
    low, high = jnp.split(terms, 2, axis=dim)
    return (low.astype(jnp.float32) + swap(high, "ctx", 1).astype(jnp.float32)).astype(
        jnp.bfloat16
    )


def scatter_chips(terms, dim):
    parts = jnp.split(terms, chip_count(), axis=dim)
    got = [parts[0]] + [swap(parts[k], "ctx", 2 * k) for k in range(1, len(parts))]
    return tree_sum([piece.astype(jnp.float32) for piece in got]).astype(jnp.bfloat16)


def scatter_shard(terms, dim):
    parts = jnp.split(terms, lax.axis_size("shard"), axis=dim)
    got = [parts[0]] + [swap(parts[j], "shard", j) for j in range(1, len(parts))]
    return tree_sum([piece.astype(jnp.float32) for piece in got])


def gather_weight(piece):
    return gather_cores(gather_chips(gather_shard(piece, -1), -2), -2)


def scatter_weight(terms):
    return scatter_shard(scatter_chips(scatter_cores(terms, -2), -2), -1)


def reduce_small(values):
    values = values + swap(values, "ctx", 1)
    values = tree_sum(
        [values] + [swap(values, "ctx", 2 * k) for k in range(1, chip_count())]
    )
    return tree_sum(
        [values] + [swap(values, "shard", j) for j in range(1, lax.axis_size("shard"))]
    )


def relative_ctx(index):
    chips = chip_count()
    return lax.axis_index("ctx") ^ ((index % chips) * 2 + index // chips)


def one_hot(source):
    size = source.shape[0]
    return (jnp.arange(size, dtype=jnp.int32)[:, None] == source[None, :]).astype(jnp.bfloat16)


def nn(left, right):
    return jnp.dot(left, right, preferred_element_type=jnp.float32)


def nt(left, right):
    return lax.dot_general(
        left, right, (((1,), (1,)), ((), ())), preferred_element_type=jnp.float32
    )


def tn(left, right):
    return lax.dot_general(
        left, right, (((0,), (0,)), ((), ())), preferred_element_type=jnp.float32
    )


def stack_heads(rows, half_len):
    return jnp.concatenate(
        [
            rows[side * half_len : (side + 1) * half_len, h * HEAD : (h + 1) * HEAD]
            for side in range(2)
            for h in range(HEADS)
        ],
        axis=0,
    )


def key_block(kv_ref, table_ref, block_index, shard_size, part):
    half_blocks = table_ref.shape[0] - 2
    high = (block_index >= half_blocks).astype(jnp.int32)
    at = table_ref[jnp.where(high == 1, 2 * half_blocks - 1 - block_index, block_index)]
    piece = kv_ref[pl.ds(at * shard_size, shard_size), high, :, part * HEAD : (part + 1) * HEAD]
    return piece.reshape(piece.shape[0] * piece.shape[1], HEAD)


def forward_kernel(table_ref, query_ref, kv_ref, out_ref, log_ref, q_s, acc_s, sum_s):
    half_blocks = table_ref.shape[0] - 2
    shard_size = kv_ref.shape[0] // half_blocks
    half_len = kv_ref.shape[2]
    block_len = shard_size * half_len
    side_rows = half_len * HEADS
    own_block = table_ref[half_blocks]
    own_shard = table_ref[half_blocks + 1]
    far_block = 2 * half_blocks - 1 - own_block
    q_s[...] = stack_heads(query_ref[...], half_len)
    acc_s[...] = jnp.zeros_like(acc_s)
    sum_s[...] = jnp.zeros_like(sum_s)

    def attend(block_index, start, count):
        keys = key_block(kv_ref, table_ref, block_index, shard_size, 0)
        values = key_block(kv_ref, table_ref, block_index, shard_size, 1)
        scores = nt(q_s[start : start + count, :], keys) * score_scale
        key_i = lax.broadcasted_iota(jnp.int32, (1, block_len), 1)
        key_at = (
            block_index * block_len
            + ((key_i // half_len) ^ own_shard) * half_len
            + key_i % half_len
        )
        row_i = start + lax.broadcasted_iota(jnp.int32, (count, 1), 0)
        query_at = (
            jnp.where(row_i >= side_rows, far_block, own_block) * block_len
            + own_shard * half_len
            + row_i % half_len
        )
        weights = jnp.where(key_at <= query_at, jnp.exp(scores), 0.0)
        sum_s[start : start + count, :] += jnp.sum(weights, axis=-1, keepdims=True)
        acc_s[start : start + count, :] += nn(weights.astype(jnp.bfloat16), values)

    def both(block_index, carry):
        attend(block_index, 0, 2 * side_rows)
        return carry

    def far_only(block_index, carry):
        attend(block_index, side_rows, side_rows)
        return carry

    lax.fori_loop(0, own_block + 1, both, 0)
    lax.fori_loop(own_block + 1, far_block + 1, far_only, 0)
    total = sum_s[...]
    result = acc_s[...] / total
    log_ref[...] = jnp.log(total)
    for side in range(2):
        for h in range(HEADS):
            at = (side * HEADS + h) * half_len
            out_ref[side * half_len : (side + 1) * half_len, h * HEAD : (h + 1) * HEAD] = result[
                at : at + half_len, :
            ]


def backward_kernel(
    table_ref, query_ref, kv_ref, out_ref, grad_ref, log_ref, dq_ref, dkv_ref, q_s, do_s, acc_s
):
    half_blocks = table_ref.shape[0] - 2
    shard_size = kv_ref.shape[0] // half_blocks
    half_len = kv_ref.shape[2]
    block_len = shard_size * half_len
    side_rows = half_len * HEADS
    own_block = table_ref[half_blocks]
    own_shard = table_ref[half_blocks + 1]
    far_block = 2 * half_blocks - 1 - own_block
    q_s[...] = stack_heads(query_ref[...], half_len)
    grads = stack_heads(grad_ref[...], half_len)
    do_s[...] = grads
    outs = stack_heads(out_ref[...], half_len)
    delta_all = jnp.transpose(
        jnp.sum(grads.astype(jnp.float32) * outs, axis=-1, keepdims=True)
    )
    log_all = jnp.transpose(log_ref[...])
    acc_s[...] = jnp.zeros_like(acc_s)

    def attend(block_index, start, count):
        high = (block_index >= half_blocks).astype(jnp.int32)
        at = table_ref[jnp.where(high == 1, 2 * half_blocks - 1 - block_index, block_index)]
        keys = key_block(kv_ref, table_ref, block_index, shard_size, 0)
        values = key_block(kv_ref, table_ref, block_index, shard_size, 1)
        queries = q_s[start : start + count, :]
        grad_rows = do_s[start : start + count, :]
        scores = nt(keys, queries) * score_scale
        key_i = lax.broadcasted_iota(jnp.int32, (block_len, 1), 0)
        key_at = (
            block_index * block_len
            + ((key_i // half_len) ^ own_shard) * half_len
            + key_i % half_len
        )
        row_i = start + lax.broadcasted_iota(jnp.int32, (1, count), 1)
        query_at = (
            jnp.where(row_i >= side_rows, far_block, own_block) * block_len
            + own_shard * half_len
            + row_i % half_len
        )
        weights = jnp.where(
            key_at <= query_at, jnp.exp(scores - log_all[:, start : start + count]), 0.0
        )
        grad_weights = nt(values, grad_rows)
        grad_scores = (weights * (grad_weights - delta_all[:, start : start + count])).astype(
            jnp.bfloat16
        )
        acc_s[start : start + count, :] += tn(grad_scores, keys)
        dk = nn(grad_scores, queries) * score_scale
        dv = nn(weights.astype(jnp.bfloat16), grad_rows)
        shape = (shard_size, half_len, HEAD)
        dkv_ref[pl.ds(at * shard_size, shard_size), high, :, :HEAD] = dk.astype(
            jnp.bfloat16
        ).reshape(shape)
        dkv_ref[pl.ds(at * shard_size, shard_size), high, :, HEAD:] = dv.astype(
            jnp.bfloat16
        ).reshape(shape)

    def both(block_index, carry):
        attend(block_index, 0, 2 * side_rows)
        return carry

    def far_only(block_index, carry):
        attend(block_index, side_rows, side_rows)
        return carry

    def none(block_index, carry):
        at = table_ref[2 * half_blocks - 1 - block_index]
        dkv_ref[pl.ds(at * shard_size, shard_size), 1] = jnp.zeros(
            (shard_size, half_len, 2 * HEAD), jnp.bfloat16
        )
        return carry

    lax.fori_loop(0, own_block + 1, both, 0)
    lax.fori_loop(own_block + 1, far_block + 1, far_only, 0)
    lax.fori_loop(far_block + 1, 2 * half_blocks, none, 0)
    result = acc_s[...] * score_scale
    for side in range(2):
        for h in range(HEADS):
            at = (side * HEADS + h) * half_len
            dq_ref[side * half_len : (side + 1) * half_len, h * HEAD : (h + 1) * HEAD] = result[
                at : at + half_len, :
            ]


def whole_spec(space=pltpu.VMEM):
    return pl.BlockSpec(memory_space=space)


def attention_forward(table, queries, kv):
    rows = queries.shape[0] * HEADS
    room = kv.size * 2 + (24 << 20)
    return pl.pallas_call(
        forward_kernel,
        out_shape=(
            jax.ShapeDtypeStruct(queries.shape, jnp.float32),
            jax.ShapeDtypeStruct((rows, 1), jnp.float32),
        ),
        in_specs=[whole_spec(pltpu.SMEM), whole_spec(), whole_spec()],
        out_specs=(whole_spec(), whole_spec()),
        scratch_shapes=[
            pltpu.VMEM((rows, HEAD), jnp.bfloat16),
            pltpu.VMEM((rows, HEAD), jnp.float32),
            pltpu.VMEM((rows, 1), jnp.float32),
        ],
        compiler_params=pltpu.CompilerParams(vmem_limit_bytes=room),
        name="attention_forward",
    )(table, queries, kv)


def attention_backward(table, queries, kv, outs, grads, logs):
    rows = queries.shape[0] * HEADS
    room = kv.size * 4 + (24 << 20)
    return pl.pallas_call(
        backward_kernel,
        out_shape=(
            jax.ShapeDtypeStruct(queries.shape, jnp.float32),
            jax.ShapeDtypeStruct(kv.shape, jnp.bfloat16),
        ),
        in_specs=[whole_spec(pltpu.SMEM)] + [whole_spec()] * 5,
        out_specs=(whole_spec(), whole_spec()),
        scratch_shapes=[
            pltpu.VMEM((rows, HEAD), jnp.bfloat16),
            pltpu.VMEM((rows, HEAD), jnp.bfloat16),
            pltpu.VMEM((rows, HEAD), jnp.float32),
        ],
        compiler_params=pltpu.CompilerParams(vmem_limit_bytes=room),
        name="attention_backward",
    )(table, queries, kv, outs, grads, logs)


def shards(
    tokens,
    positions,
    cotangent,
    query_weight,
    query_first,
    query_second,
    keyval_weight,
    keyval_first,
    keyval_second,
    output_weight,
    output_first,
    output_second,
    gateup_weight,
    gateup_first,
    gateup_second,
    down_weight,
    down_first,
    down_second,
    norm_scales,
    norm_first,
    norm_second,
    head_scales,
    head_first,
    head_second,
):
    bfloat = jnp.bfloat16
    single = jnp.float32
    ctx_size = lax.axis_size("ctx")
    shard_size = lax.axis_size("shard")
    ctx_at = lax.axis_index("ctx")
    shard_at = lax.axis_index("shard")
    row_count, width = tokens.shape
    half_len = row_count // 2
    block_len = half_len * shard_size
    piece_len = width // ctx_size
    slice_len = HEAD // shard_size

    keyval_full = gather_weight(
        jnp.concatenate([keyval_weight[0], keyval_weight[1]], axis=-1).astype(bfloat)
    )
    attn_full = gather_weight(
        jnp.stack([query_weight.astype(bfloat), output_weight.astype(bfloat).T])
    )
    ffn_full = gather_weight(
        jnp.stack(
            [
                gateup_weight[0].astype(bfloat),
                gateup_weight[1].astype(bfloat),
                down_weight.astype(bfloat).T,
            ]
        )
    )
    query_full, output_full = (attn_full[0], attn_full[1])
    gate_full, up_full, down_full = (ffn_full[0], ffn_full[1], ffn_full[2])

    feature = jnp.arange(width, dtype=jnp.int32)
    feature_map = one_hot(relative_ctx(feature // piece_len) * piece_len + feature % piece_len)
    channel = jnp.arange(2 * HEAD, dtype=jnp.int32)
    channel_map = one_hot(
        ((channel % HEAD) // slice_len ^ shard_at) * (2 * slice_len)
        + (channel // HEAD) * slice_len
        + channel % slice_len
    )
    keyval_sorted = nn(keyval_full, channel_map).astype(bfloat)

    scales = lax.dot_general(
        norm_scales,
        feature_map.astype(single),
        (((1,), (0,)), ((), ())),
        precision=lax.Precision.HIGHEST,
        preferred_element_type=single,
    )
    inputs = nn(tokens, feature_map)
    upstream = nn(cotangent, feature_map)

    own_at = lax.dynamic_slice_in_dim(
        positions, (ctx_at * shard_size + shard_at) * row_count, row_count
    )
    first_at = positions.reshape(ctx_size, shard_size * row_count)[:, 0] // block_len
    rel = jnp.arange(ctx_size, dtype=jnp.int32)
    blocks_rel = jnp.sum(
        jnp.where(relative_ctx(rel)[:, None] == rel[None, :], first_at[None, :], 0), axis=1
    )
    places = jnp.sum(
        jnp.where(blocks_rel[None, :] == rel[:, None], rel[None, :], 0), axis=1
    )
    table = jnp.concatenate(
        [places, blocks_rel[:1], jnp.full((1,), shard_at, jnp.int32)]
    ).astype(jnp.int32)

    normed_in, inverse_in = rms_forward(inputs)
    attn_in = (normed_in * (1.0 + scales[0])).astype(bfloat)
    cosine, sine = rope_tables(own_at)
    keyval_proj = nn(attn_in, keyval_sorted)
    key_normed, key_inverse = rms_forward(keyval_proj[:, :HEAD])
    key_scaled = key_normed * (1.0 + head_scales[1])
    keys_own = (key_scaled * cosine + rotate(key_scaled) * sine).astype(bfloat)
    values_own = keyval_proj[:, HEAD:].astype(bfloat)
    kv_own = jnp.concatenate([keys_own, values_own], axis=-1).reshape(
        1, 2, half_len, 2 * HEAD
    )
    kv_all = gather_cores(gather_chips(gather_shard(kv_own, 0), 0), 0)

    query_proj = nn(attn_in, query_full)
    query_normed, query_inverse = rms_forward(query_proj.reshape(row_count, HEADS, HEAD))
    query_scaled = query_normed * (1.0 + head_scales[0])
    query_rows = (
        (query_scaled * cosine[:, None, :] + rotate(query_scaled) * sine[:, None, :])
        .astype(bfloat)
        .reshape(row_count, HEADS * HEAD)
    )
    attn_rows, attn_logs = attention_forward(table, query_rows, kv_all)
    attn_b = attn_rows.astype(bfloat)
    attn_out = nt(attn_b, output_full)
    out_normed, out_inverse = rms_forward(attn_out)
    hidden_in = inputs + out_normed * (1.0 + scales[1])
    mid_normed, mid_inverse = rms_forward(hidden_in)
    ffn_in = (mid_normed * (1.0 + scales[2])).astype(bfloat)
    gate_pre = nn(ffn_in, gate_full)
    up_pre = nn(ffn_in, up_full)
    gate_value, gate_slope = gelu_parts(gate_pre)
    hidden_b = (gate_value * up_pre).astype(bfloat)
    ffn_out = nt(hidden_b, down_full)
    ffn_normed, ffn_inverse = rms_forward(ffn_out)
    block_out = nt(
        (hidden_in + ffn_normed * (1.0 + scales[3])).astype(bfloat), feature_map
    ).astype(bfloat)
    grad_norm3 = jnp.sum(upstream * ffn_normed, axis=0)
    ffn_grad = rms_backward(ffn_normed, ffn_inverse, upstream * (1.0 + scales[3])).astype(bfloat)
    down_wgrad = tn(ffn_grad, hidden_b).astype(bfloat)
    hidden_grad = nn(ffn_grad, down_full)
    gate_grad = (hidden_grad * up_pre * gate_slope).astype(bfloat)
    up_grad = (hidden_grad * gate_value).astype(bfloat)
    gate_wgrad = tn(ffn_in, gate_grad).astype(bfloat)
    up_wgrad = tn(ffn_in, up_grad).astype(bfloat)
    ffn_owned = scatter_weight(jnp.stack([gate_wgrad, up_wgrad, down_wgrad]))
    ffn_in_grad = nt(gate_grad, gate_full) + nt(up_grad, up_full)
    grad_norm2 = jnp.sum(ffn_in_grad * mid_normed, axis=0)
    residual_grad = upstream + rms_backward(mid_normed, mid_inverse, ffn_in_grad * (1.0 + scales[2]))
    grad_norm1 = jnp.sum(residual_grad * out_normed, axis=0)
    attn_out_grad = rms_backward(
        out_normed, out_inverse, residual_grad * (1.0 + scales[1])
    ).astype(bfloat)
    output_wgrad = tn(attn_out_grad, attn_b).astype(bfloat)
    attn_grad_b = nn(attn_out_grad, output_full).astype(bfloat)
    query_parts, kv_terms = attention_backward(
        table, query_rows, kv_all, attn_rows, attn_grad_b, attn_logs
    )
    kv_grad = scatter_shard(scatter_chips(scatter_cores(kv_terms, 0), 0), 0).reshape(
        row_count, 2 * HEAD
    )
    query_rot_grad = query_parts.reshape(row_count, HEADS, HEAD)
    query_rope_grad = query_rot_grad * cosine[:, None, :] + rotate_back(
        query_rot_grad * sine[:, None, :]
    )
    grad_head0 = jnp.sum(query_rope_grad * query_normed, axis=(0, 1))
    query_proj_grad = (
        rms_backward(query_normed, query_inverse, query_rope_grad * (1.0 + head_scales[0]))
        .reshape(row_count, HEADS * HEAD)
        .astype(bfloat)
    )
    query_wgrad = tn(attn_in, query_proj_grad).astype(bfloat)
    attn_owned = scatter_weight(jnp.stack([query_wgrad, output_wgrad]))
    key_rot_grad = kv_grad[:, :HEAD]
    value_grad = kv_grad[:, HEAD:]
    key_rope_grad = key_rot_grad * cosine + rotate_back(key_rot_grad * sine)
    grad_head1 = jnp.sum(key_rope_grad * key_normed, axis=0)
    key_proj_grad = rms_backward(
        key_normed, key_inverse, key_rope_grad * (1.0 + head_scales[1])
    ).astype(bfloat)
    keyval_proj_grad = jnp.concatenate([key_proj_grad, value_grad.astype(bfloat)], axis=-1)
    keyval_wgrad = nt(tn(attn_in, keyval_proj_grad).astype(bfloat), channel_map).astype(bfloat)
    keyval_owned = scatter_weight(keyval_wgrad)
    attn_in_grad = nt(query_proj_grad, query_full) + nt(keyval_proj_grad, keyval_sorted)
    grad_norm0 = jnp.sum(attn_in_grad * normed_in, axis=0)
    tokens_grad = nt(
        (
            residual_grad
            + rms_backward(normed_in, inverse_in, attn_in_grad * (1.0 + scales[0]))
        ).astype(bfloat),
        feature_map,
    ).astype(bfloat)
    norm_terms = lax.dot_general(
        jnp.stack([grad_norm0, grad_norm1, grad_norm2, grad_norm3]),
        feature_map.astype(single),
        (((1,), (1,)), ((), ())),
        precision=lax.Precision.HIGHEST,
        preferred_element_type=single,
    )
    small = reduce_small(
        jnp.concatenate([norm_terms.reshape(-1), grad_head0, grad_head1]).reshape(-1, 128)
    ).reshape(-1)
    norm_wgrad = small[: 4 * width].reshape(4, width)
    head_wgrad = small[4 * width :].reshape(2, HEAD)

    query_set = adam_update(query_weight, query_first, query_second, attn_owned[0])
    keyval_set = adam_update(
        keyval_weight,
        keyval_first,
        keyval_second,
        jnp.stack([keyval_owned[:, :slice_len], keyval_owned[:, slice_len:]]),
    )
    output_set = adam_update(output_weight, output_first, output_second, attn_owned[1].T)
    gateup_set = adam_update(gateup_weight, gateup_first, gateup_second, ffn_owned[:2])
    down_set = adam_update(down_weight, down_first, down_second, ffn_owned[2].T)
    norm_set = adam_update(norm_scales, norm_first, norm_second, norm_wgrad)
    head_set = adam_update(head_scales, head_first, head_second, head_wgrad)
    return (
        (block_out, tokens_grad)
        + query_set
        + keyval_set
        + output_set
        + gateup_set
        + down_set
        + norm_set
        + head_set
    )


def solution(mesh):
    placed = (
        P(("ctx", "shard"), None),
        P(),
        P(("ctx", "shard"), None),
        P("ctx", "shard"),
        P("ctx", "shard"),
        P("ctx", "shard"),
        P(None, "ctx", "shard"),
        P(None, "ctx", "shard"),
        P(None, "ctx", "shard"),
        P("shard", "ctx"),
        P("shard", "ctx"),
        P("shard", "ctx"),
        P(None, "ctx", "shard"),
        P(None, "ctx", "shard"),
        P(None, "ctx", "shard"),
        P("shard", "ctx"),
        P("shard", "ctx"),
        P("shard", "ctx"),
        P(),
        P(),
        P(),
        P(),
        P(),
        P(),
    )
    return jax.shard_map(
        shards,
        mesh=mesh,
        in_specs=placed,
        out_specs=(
            P(("ctx", "shard"), None),
            P(("ctx", "shard"), None),
            P("ctx", "shard"),
            P("ctx", "shard"),
            P("ctx", "shard"),
            P("ctx", "shard"),
            P(None, "ctx", "shard"),
            P(None, "ctx", "shard"),
            P(None, "ctx", "shard"),
            P(None, "ctx", "shard"),
            P("shard", "ctx"),
            P("shard", "ctx"),
            P("shard", "ctx"),
            P("shard", "ctx"),
            P(None, "ctx", "shard"),
            P(None, "ctx", "shard"),
            P(None, "ctx", "shard"),
            P(None, "ctx", "shard"),
            P("shard", "ctx"),
            P("shard", "ctx"),
            P("shard", "ctx"),
            P("shard", "ctx"),
            P(),
            P(),
            P(),
            P(),
            P(),
            P(),
            P(),
            P(),
        ),
        check_vma=False,
    )
```

```python
import jax
import jax.numpy as jnp
from jax import lax
from jax.experimental import pallas as pl
from jax.experimental.pallas import tpu as pltpu
from jax.sharding import PartitionSpec as P

HEADS = 4
HEAD = 256
STEP = 3


norm_eps = 1e-06
rope_base = 1000000.0
score_scale = 0.0625
learn_rate = 0.02
beta_first = 0.9
beta_second = 0.95
adam_eps = 1e-08
weight_decay = 0.1
gelu_coef = 0.7978845608028654
masked_value = -1e30


def rms_forward(values):
    inverse = lax.rsqrt(jnp.mean(values * values, axis=-1, keepdims=True) + norm_eps)
    return (values * inverse, inverse)


def rms_backward(normed, inverse, upstream):
    return inverse * (upstream - normed * jnp.mean(upstream * normed, axis=-1, keepdims=True))


def rotate(values):
    middle = values.shape[-1] // 2
    return jnp.concatenate([-values[..., middle:], values[..., :middle]], axis=-1)


def rotate_back(values):
    middle = values.shape[-1] // 2
    return jnp.concatenate([values[..., middle:], -values[..., :middle]], axis=-1)


def rope_tables(places):
    middle = HEAD // 2
    freqs = rope_base ** (-(jnp.arange(middle, dtype=jnp.float32) * 2.0 / HEAD))
    angles = places.astype(jnp.float32)[:, None] * freqs[None, :]
    cosine = jnp.cos(angles)
    sine = jnp.sin(angles)
    return (jnp.concatenate([cosine, cosine], axis=-1), jnp.concatenate([sine, sine], axis=-1))


def gelu_parts(values):
    inner = gelu_coef * (values + 0.044715 * values * values * values)
    tangent = jnp.tanh(inner)
    result = 0.5 * values * (1.0 + tangent)
    slope = 0.5 * (1.0 + tangent) + 0.5 * values * (1.0 - tangent * tangent) * gelu_coef * (
        1.0 + 3.0 * 0.044715 * values * values
    )
    return (result, slope)


def adam_update(weight, first, second, grad):
    first_new = beta_first * first + (1.0 - beta_first) * grad
    second_new = beta_second * second + (1.0 - beta_second) * grad * grad
    first_hat = first_new / (1.0 - beta_first**STEP)
    second_hat = second_new / (1.0 - beta_second**STEP)
    weight_new = weight - learn_rate * (
        first_hat / (jnp.sqrt(second_hat) + adam_eps) + weight_decay * weight
    )
    return (grad, weight_new, first_new, second_new)


def swap(piece, axis, distance):
    return lax.ppermute(piece, axis, [(i, i ^ distance) for i in range(lax.axis_size(axis))])


def chip_count():
    return lax.axis_size("ctx") // 2


def gather_shard(piece, dim):
    return jnp.concatenate(
        [piece] + [swap(piece, "shard", j) for j in range(1, lax.axis_size("shard"))], axis=dim
    )


def gather_chips(piece, dim):
    return jnp.concatenate(
        [piece] + [swap(piece, "ctx", 2 * k) for k in range(1, chip_count())], axis=dim
    )


def gather_cores(piece, dim):
    return jnp.concatenate([piece, swap(piece, "ctx", 1)], axis=dim)


def tree_sum(terms):
    while len(terms) > 1:
        terms = [terms[i] + terms[i + 1] for i in range(0, len(terms), 2)]
    return terms[0]


def wide_sum(terms):
    return tree_sum([piece.astype(jnp.float32) for piece in terms])


def scatter_cores(terms, dim):
    keep = lax.index_in_dim(terms, 0, dim, keepdims=False)
    send = lax.index_in_dim(terms, 1, dim, keepdims=False)
    return wide_sum([keep, swap(send, "ctx", 1)])


def scatter_chips(terms, dim):
    parts = jnp.split(terms, chip_count(), axis=dim)
    return wide_sum([parts[0]] + [swap(parts[k], "ctx", 2 * k) for k in range(1, len(parts))])


def scatter_shard(terms, dim):
    parts = jnp.split(terms, lax.axis_size("shard"), axis=dim)
    return wide_sum([parts[0]] + [swap(parts[j], "shard", j) for j in range(1, len(parts))])


def gather_rows(piece):
    rows = gather_chips(piece, -2)
    split = rows.reshape(rows.shape[:-2] + (chip_count(), 1, piece.shape[-2], rows.shape[-1]))
    return gather_cores(split, -3).reshape(
        rows.shape[:-2] + (2 * rows.shape[-2], rows.shape[-1])
    )


def scatter_rows(terms):
    chips = chip_count()
    rows = terms.shape[-2] // (2 * chips)
    split = terms.reshape(terms.shape[:-2] + (chips, 2, rows, terms.shape[-1]))
    summed = scatter_cores(split, split.ndim - 3).astype(jnp.bfloat16)
    return scatter_chips(summed.reshape(terms.shape[:-2] + (chips * rows, terms.shape[-1])), -2)


def scatter_weight(terms):
    return scatter_shard(scatter_rows(terms).astype(jnp.bfloat16), -1)


def reduce_small(values):
    for axis in ("ctx", "shard"):
        distance = 1
        while distance < lax.axis_size(axis):
            values = values + swap(values, axis, distance)
            distance *= 2
    return values


def relative_ctx(index):
    return lax.axis_index("ctx") ^ index


def one_hot(source):
    size = source.shape[0]
    return (jnp.arange(size, dtype=jnp.int32)[:, None] == source[None, :]).astype(jnp.bfloat16)


def nn(left, right):
    return jnp.dot(left, right, preferred_element_type=jnp.float32)


def nt(left, right):
    return lax.dot_general(
        left, right, (((1,), (1,)), ((), ())), preferred_element_type=jnp.float32
    )


def tn(left, right):
    return lax.dot_general(
        left, right, (((0,), (0,)), ((), ())), preferred_element_type=jnp.float32
    )


def stack_heads(rows, half_len):
    return jnp.concatenate(
        [
            rows[side * half_len : (side + 1) * half_len, h * HEAD : (h + 1) * HEAD]
            for side in range(2)
            for h in range(HEADS)
        ],
        axis=0,
    )


def key_block(kv_ref, table_ref, block_index, shard_size, part):
    half_blocks = table_ref.shape[0] - 2
    high = (block_index >= half_blocks).astype(jnp.int32)
    at = table_ref[jnp.where(high == 1, 2 * half_blocks - 1 - block_index, block_index)]
    piece = kv_ref[pl.ds(at * shard_size, shard_size), high, :, part * HEAD : (part + 1) * HEAD]
    return piece.reshape(piece.shape[0] * piece.shape[1], HEAD)


def forward_kernel(table_ref, query_ref, kv_ref, out_ref, log_ref, q_s, acc_s, sum_s):
    half_blocks = table_ref.shape[0] - 2
    shard_size = kv_ref.shape[0] // half_blocks
    half_len = kv_ref.shape[2]
    block_len = shard_size * half_len
    side_rows = half_len * HEADS
    own_block = table_ref[half_blocks]
    own_shard = table_ref[half_blocks + 1]
    far_block = 2 * half_blocks - 1 - own_block
    q_s[...] = stack_heads(query_ref[...], half_len)
    acc_s[...] = jnp.zeros_like(acc_s)
    sum_s[...] = jnp.zeros_like(sum_s)
    key_i = lax.broadcasted_iota(jnp.int32, (1, block_len), 1)
    key_in = ((key_i // half_len) ^ own_shard) * half_len + key_i % half_len
    row_i = lax.broadcasted_iota(jnp.int32, (side_rows, 1), 0)
    query_in = own_shard * half_len + row_i % half_len
    offset_in = key_in - query_in

    def attend(unit):
        far = (unit > own_block).astype(jnp.int32)
        block_index = unit - far * (own_block + 1)
        query_block = jnp.where(far == 1, far_block, own_block)
        rows = pl.ds(pl.multiple_of(far * side_rows, side_rows), side_rows)
        keys = key_block(kv_ref, table_ref, block_index, shard_size, 0)
        values = key_block(kv_ref, table_ref, block_index, shard_size, 1)
        scores = nt(q_s[rows, :], keys) * score_scale
        visible = offset_in <= (query_block - block_index) * block_len
        weights = jnp.where(visible, jnp.exp(scores), 0.0)
        return (
            rows,
            jnp.sum(weights, axis=-1, keepdims=True),
            nn(weights.astype(jnp.bfloat16), values),
        )

    def attend_some(first, count):
        for rows, total, mixed in [attend(first + i) for i in range(count)]:
            sum_s[rows, :] += total
            acc_s[rows, :] += mixed

    unit_count = 2 * half_blocks + 1
    group = 4

    def attend_group(index, carry):
        attend_some(index * group, group)
        return carry

    lax.fori_loop(0, unit_count // group, attend_group, 0)
    attend_some(unit_count - unit_count % group, unit_count % group)
    total = sum_s[...]
    result = acc_s[...] / total
    log_ref[...] = jnp.log(total)
    for side in range(2):
        for h in range(HEADS):
            at = (side * HEADS + h) * half_len
            out_ref[side * half_len : (side + 1) * half_len, h * HEAD : (h + 1) * HEAD] = result[
                at : at + half_len, :
            ]


def backward_kernel(
    table_ref,
    query_ref,
    kv_ref,
    out_ref,
    grad_ref,
    log_ref,
    dq_ref,
    dkv_ref,
    q_s,
    do_s,
    acc_s,
    log_s,
    delta_s,
):
    half_blocks = table_ref.shape[0] - 2
    shard_size = kv_ref.shape[0] // half_blocks
    half_len = kv_ref.shape[2]
    block_len = shard_size * half_len
    side_rows = half_len * HEADS
    own_block = table_ref[half_blocks]
    own_shard = table_ref[half_blocks + 1]
    far_block = 2 * half_blocks - 1 - own_block
    q_s[...] = stack_heads(query_ref[...], half_len)
    grads = stack_heads(grad_ref[...], half_len)
    do_s[...] = grads
    outs = stack_heads(out_ref[...], half_len)
    delta_all = jnp.transpose(
        jnp.sum(grads.astype(jnp.float32) * outs, axis=-1, keepdims=True)
    )
    log_all = jnp.transpose(log_ref[...])
    acc_s[...] = jnp.zeros_like(acc_s)
    shape = (shard_size, half_len, HEAD)
    for side in range(2):
        log_s[side] = log_all[:, side * side_rows : (side + 1) * side_rows]
        delta_s[side] = delta_all[:, side * side_rows : (side + 1) * side_rows]
    key_i = lax.broadcasted_iota(jnp.int32, (block_len, 1), 0)
    key_in = ((key_i // half_len) ^ own_shard) * half_len + key_i % half_len
    row_i = lax.broadcasted_iota(jnp.int32, (1, side_rows), 1)
    query_in = own_shard * half_len + row_i % half_len
    offset_in = key_in - query_in

    def attend(unit):
        far = (unit > own_block).astype(jnp.int32)
        block_index = unit - far * (own_block + 1)
        query_block = jnp.where(far == 1, far_block, own_block)
        rows = pl.ds(pl.multiple_of(far * side_rows, side_rows), side_rows)
        high = (block_index >= half_blocks).astype(jnp.int32)
        at = table_ref[jnp.where(high == 1, 2 * half_blocks - 1 - block_index, block_index)]
        keys = key_block(kv_ref, table_ref, block_index, shard_size, 0)
        values = key_block(kv_ref, table_ref, block_index, shard_size, 1)
        queries = q_s[rows, :]
        grad_rows = do_s[rows, :]
        scores = nt(keys, queries) * score_scale
        visible = offset_in <= (query_block - block_index) * block_len
        weights = jnp.where(visible, jnp.exp(scores - log_s[far]), 0.0)
        grad_weights = nt(values, grad_rows)
        grad_scores = (weights * (grad_weights - delta_s[far])).astype(jnp.bfloat16)
        dq = tn(grad_scores, keys)
        dk = nn(grad_scores, queries) * score_scale
        dv = nn(weights.astype(jnp.bfloat16), grad_rows)
        seen = jnp.logical_and(far == 1, block_index <= own_block)
        return (rows, pl.ds(at * shard_size, shard_size), high, seen, dq, dk, dv)

    def attend_some(first, count):
        for rows, devices, high, seen, dq, dk, dv in [attend(first + i) for i in range(count)]:
            acc_s[rows, :] += dq
            for part, value in enumerate((dk, dv)):
                columns = slice(part * HEAD, (part + 1) * HEAD)
                old = dkv_ref[devices, high, :, columns].astype(jnp.float32)
                dkv_ref[devices, high, :, columns] = (
                    value.reshape(shape) + jnp.where(seen, old, 0.0)
                ).astype(jnp.bfloat16)

    def none(block_index, carry):
        at = table_ref[2 * half_blocks - 1 - block_index]
        dkv_ref[pl.ds(at * shard_size, shard_size), 1] = jnp.zeros(
            (shard_size, half_len, 2 * HEAD), jnp.bfloat16
        )
        return carry

    unit_count = 2 * half_blocks + 1
    group = 4

    def attend_group(index, carry):
        attend_some(index * group, group)
        return carry

    lax.fori_loop(0, unit_count // group, attend_group, 0)
    attend_some(unit_count - unit_count % group, unit_count % group)
    lax.fori_loop(far_block + 1, 2 * half_blocks, none, 0)
    result = acc_s[...] * score_scale
    for side in range(2):
        for h in range(HEADS):
            at = (side * HEADS + h) * half_len
            dq_ref[side * half_len : (side + 1) * half_len, h * HEAD : (h + 1) * HEAD] = result[
                at : at + half_len, :
            ]


def whole_spec(space=pltpu.VMEM):
    return pl.BlockSpec(memory_space=space)


def attention_forward(table, queries, kv):
    rows = queries.shape[0] * HEADS
    room = kv.size * 2 + (24 << 20)
    return pl.pallas_call(
        forward_kernel,
        out_shape=(
            jax.ShapeDtypeStruct(queries.shape, jnp.float32),
            jax.ShapeDtypeStruct((rows, 1), jnp.float32),
        ),
        in_specs=[whole_spec(pltpu.SMEM), whole_spec(), whole_spec()],
        out_specs=(whole_spec(), whole_spec()),
        scratch_shapes=[
            pltpu.VMEM((rows, HEAD), jnp.bfloat16),
            pltpu.VMEM((rows, HEAD), jnp.float32),
            pltpu.VMEM((rows, 1), jnp.float32),
        ],
        compiler_params=pltpu.CompilerParams(vmem_limit_bytes=room),
        cost_estimate=pl.CostEstimate(
            flops=12 * rows * kv.size, transcendentals=0, bytes_accessed=8 * kv.size
        ),
        name="attention_forward",
    )(table, queries, kv)


def attention_backward(table, queries, kv, outs, grads, logs):
    rows = queries.shape[0] * HEADS
    room = kv.size * 4 + (24 << 20)
    return pl.pallas_call(
        backward_kernel,
        out_shape=(
            jax.ShapeDtypeStruct(queries.shape, jnp.float32),
            jax.ShapeDtypeStruct(kv.shape, jnp.bfloat16),
        ),
        in_specs=[whole_spec(pltpu.SMEM)] + [whole_spec()] * 5,
        out_specs=(whole_spec(), whole_spec()),
        scratch_shapes=[
            pltpu.VMEM((rows, HEAD), jnp.bfloat16),
            pltpu.VMEM((rows, HEAD), jnp.bfloat16),
            pltpu.VMEM((rows, HEAD), jnp.float32),
            pltpu.VMEM((2, 1, rows // 2), jnp.float32),
            pltpu.VMEM((2, 1, rows // 2), jnp.float32),
        ],
        compiler_params=pltpu.CompilerParams(vmem_limit_bytes=room),
        cost_estimate=pl.CostEstimate(
            flops=12 * rows * kv.size, transcendentals=0, bytes_accessed=12 * kv.size
        ),
        name="attention_backward",
    )(table, queries, kv, outs, grads, logs)


def shards(
    tokens,
    positions,
    cotangent,
    query_weight,
    query_first,
    query_second,
    keyval_weight,
    keyval_first,
    keyval_second,
    output_weight,
    output_first,
    output_second,
    gateup_weight,
    gateup_first,
    gateup_second,
    down_weight,
    down_first,
    down_second,
    norm_scales,
    norm_first,
    norm_second,
    head_scales,
    head_first,
    head_second,
):
    bfloat = jnp.bfloat16
    single = jnp.float32
    ctx_size = lax.axis_size("ctx")
    shard_size = lax.axis_size("shard")
    ctx_at = lax.axis_index("ctx")
    shard_at = lax.axis_index("shard")
    row_count, width = tokens.shape
    half_len = row_count // 2
    block_len = half_len * shard_size
    piece_len = width // ctx_size
    slice_len = HEAD // shard_size

    group_tokens = gather_shard(tokens, 0)
    attn_pieces = gather_shard(
        jnp.concatenate(
            [
                keyval_weight[0].astype(bfloat),
                keyval_weight[1].astype(bfloat),
                query_weight.astype(bfloat),
                output_weight.astype(bfloat).T,
            ],
            axis=-1,
        )[None],
        0,
    )
    ffn_full = gather_rows(
        jnp.stack(
            [
                gateup_weight[0].astype(bfloat),
                gateup_weight[1].astype(bfloat),
                down_weight.astype(bfloat).T,
            ]
        )
    )
    gate_full, up_full, down_full = (ffn_full[0], ffn_full[1], ffn_full[2])

    def side_by_side(start, size):
        return jnp.concatenate(
            [attn_pieces[j, :, start : start + size] for j in range(shard_size)], axis=-1
        )

    keyval_full = gather_rows(side_by_side(0, 2 * slice_len))
    attn_full = gather_rows(
        jnp.stack([side_by_side(2 * slice_len, HEAD), side_by_side(2 * slice_len + HEAD, HEAD)])
    )
    query_full, output_full = (attn_full[0], attn_full[1])

    feature = jnp.arange(width, dtype=jnp.int32)
    feature_map = one_hot(relative_ctx(feature // piece_len) * piece_len + feature % piece_len)
    channel = jnp.arange(2 * HEAD, dtype=jnp.int32)
    channel_map = one_hot(
        ((channel % HEAD) // slice_len ^ shard_at) * (2 * slice_len)
        + (channel // HEAD) * slice_len
        + channel % slice_len
    )
    keyval_sorted = nn(keyval_full, channel_map).astype(bfloat)

    scales = lax.dot_general(
        norm_scales,
        feature_map.astype(single),
        (((1,), (0,)), ((), ())),
        precision=lax.Precision.HIGHEST,
        preferred_element_type=single,
    )
    group_inputs = nn(group_tokens, feature_map)
    inputs = group_inputs[:row_count]
    upstream = nn(cotangent, feature_map)

    ctx_places = lax.dynamic_slice_in_dim(
        positions, ctx_at * shard_size * row_count, shard_size * row_count
    ).reshape(shard_size, row_count)
    piece = jnp.arange(shard_size, dtype=jnp.int32)
    group_at = jnp.sum(
        jnp.where(
            ((piece ^ shard_at)[:, None] == piece[None, :])[:, :, None], ctx_places[None], 0
        ),
        axis=1,
    ).reshape(-1)
    first_at = positions.reshape(ctx_size, shard_size * row_count)[:, 0] // block_len
    rel = jnp.arange(ctx_size, dtype=jnp.int32)
    blocks_rel = jnp.sum(
        jnp.where(relative_ctx(rel)[:, None] == rel[None, :], first_at[None, :], 0), axis=1
    )
    places = jnp.sum(
        jnp.where(blocks_rel[None, :] == rel[:, None], rel[None, :], 0), axis=1
    )
    table = jnp.concatenate(
        [places, blocks_rel[:1], jnp.full((1,), shard_at, jnp.int32)]
    ).astype(jnp.int32)

    group_normed, group_inverse = rms_forward(group_inputs)
    group_in = (group_normed * (1.0 + scales[0])).astype(bfloat)
    normed_in, inverse_in = (group_normed[:row_count], group_inverse[:row_count])
    attn_in = group_in[:row_count]
    group_cosine, group_sine = rope_tables(group_at)
    cosine, sine = (group_cosine[:row_count], group_sine[:row_count])
    keyval_proj = nn(group_in, keyval_sorted)
    group_key_normed, group_key_inverse = rms_forward(keyval_proj[:, :HEAD])
    key_normed, key_inverse = (group_key_normed[:row_count], group_key_inverse[:row_count])
    key_scaled = group_key_normed * (1.0 + head_scales[1])
    keys_own = (key_scaled * group_cosine + rotate(key_scaled) * group_sine).astype(bfloat)
    values_own = keyval_proj[:, HEAD:].astype(bfloat)
    kv_own = jnp.concatenate([keys_own, values_own], axis=-1).reshape(
        shard_size, 2, half_len, 2 * HEAD
    )
    kv_chips = gather_chips(kv_own, 0).reshape(-1, 1, shard_size, 2, half_len, 2 * HEAD)
    kv_all = gather_cores(kv_chips, 1).reshape(-1, 2, half_len, 2 * HEAD)

    query_proj = nn(attn_in, query_full)
    query_normed, query_inverse = rms_forward(query_proj.reshape(row_count, HEADS, HEAD))
    query_scaled = query_normed * (1.0 + head_scales[0])
    query_rows = (
        (query_scaled * cosine[:, None, :] + rotate(query_scaled) * sine[:, None, :])
        .astype(bfloat)
        .reshape(row_count, HEADS * HEAD)
    )
    attn_rows, attn_logs = attention_forward(table, query_rows, kv_all)
    attn_b = attn_rows.astype(bfloat)
    attn_out = nt(attn_b, output_full)
    out_normed, out_inverse = rms_forward(attn_out)
    hidden_in = inputs + out_normed * (1.0 + scales[1])
    mid_normed, mid_inverse = rms_forward(hidden_in)
    ffn_in = (mid_normed * (1.0 + scales[2])).astype(bfloat)
    group_ffn = gather_shard(ffn_in, 0)
    gate_pre = nn(group_ffn, gate_full)
    up_pre = nn(group_ffn, up_full)
    gate_value, gate_slope = gelu_parts(gate_pre)
    hidden_b = (gate_value * up_pre).astype(bfloat)
    ffn_out = scatter_shard(nt(hidden_b, down_full).astype(bfloat), 0)
    ffn_normed, ffn_inverse = rms_forward(ffn_out)
    block_out = nt(
        (hidden_in + ffn_normed * (1.0 + scales[3])).astype(bfloat), feature_map
    ).astype(bfloat)
    grad_norm3 = jnp.sum(upstream * ffn_normed, axis=0)
    ffn_grad = rms_backward(ffn_normed, ffn_inverse, upstream * (1.0 + scales[3])).astype(bfloat)
    group_grad = gather_shard(ffn_grad, 0)
    hidden_grad = nn(group_grad, down_full)
    gate_grad = (hidden_grad * up_pre * gate_slope).astype(bfloat)
    up_grad = (hidden_grad * gate_value).astype(bfloat)
    ffn_in_grad = scatter_shard(
        (nt(gate_grad, gate_full) + nt(up_grad, up_full)).astype(bfloat), 0
    )
    ffn_owned = scatter_rows(
        jnp.stack(
            [
                tn(group_ffn, gate_grad).astype(bfloat),
                tn(group_ffn, up_grad).astype(bfloat),
                tn(group_grad, hidden_b).astype(bfloat),
            ]
        )
    )
    grad_norm2 = jnp.sum(ffn_in_grad * mid_normed, axis=0)
    residual_grad = upstream + rms_backward(mid_normed, mid_inverse, ffn_in_grad * (1.0 + scales[2]))
    grad_norm1 = jnp.sum(residual_grad * out_normed, axis=0)
    attn_out_grad = rms_backward(
        out_normed, out_inverse, residual_grad * (1.0 + scales[1])
    ).astype(bfloat)
    output_wgrad = tn(attn_out_grad, attn_b).astype(bfloat)
    attn_grad_b = nn(attn_out_grad, output_full).astype(bfloat)
    query_parts, kv_terms = attention_backward(
        table, query_rows, kv_all, attn_rows, attn_grad_b, attn_logs
    )
    kv_terms = kv_terms.reshape(-1, 2, shard_size, 2, half_len, 2 * HEAD)
    kv_terms = scatter_cores(kv_terms, 1).astype(bfloat)
    kv_terms = scatter_chips(kv_terms, 0).astype(bfloat)[0]
    kv_grad = scatter_shard(kv_terms, 0).reshape(row_count, 2 * HEAD)
    query_rot_grad = query_parts.reshape(row_count, HEADS, HEAD)
    query_rope_grad = query_rot_grad * cosine[:, None, :] + rotate_back(
        query_rot_grad * sine[:, None, :]
    )
    grad_head0 = jnp.sum(query_rope_grad * query_normed, axis=(0, 1))
    query_proj_grad = (
        rms_backward(query_normed, query_inverse, query_rope_grad * (1.0 + head_scales[0]))
        .reshape(row_count, HEADS * HEAD)
        .astype(bfloat)
    )
    query_wgrad = tn(attn_in, query_proj_grad).astype(bfloat)
    attn_owned = scatter_weight(jnp.stack([query_wgrad, output_wgrad]))
    key_rot_grad = kv_grad[:, :HEAD]
    value_grad = kv_grad[:, HEAD:]
    key_rope_grad = key_rot_grad * cosine + rotate_back(key_rot_grad * sine)
    grad_head1 = jnp.sum(key_rope_grad * key_normed, axis=0)
    key_proj_grad = rms_backward(
        key_normed, key_inverse, key_rope_grad * (1.0 + head_scales[1])
    ).astype(bfloat)
    keyval_proj_grad = jnp.concatenate([key_proj_grad, value_grad.astype(bfloat)], axis=-1)
    keyval_wgrad = nt(tn(attn_in, keyval_proj_grad).astype(bfloat), channel_map).astype(bfloat)
    keyval_owned = scatter_weight(keyval_wgrad)
    attn_in_grad = nt(query_proj_grad, query_full) + nt(keyval_proj_grad, keyval_sorted)
    grad_norm0 = jnp.sum(attn_in_grad * normed_in, axis=0)
    tokens_grad = nt(
        (
            residual_grad
            + rms_backward(normed_in, inverse_in, attn_in_grad * (1.0 + scales[0]))
        ).astype(bfloat),
        feature_map,
    ).astype(bfloat)
    norm_terms = lax.dot_general(
        jnp.stack([grad_norm0, grad_norm1, grad_norm2, grad_norm3]),
        feature_map.astype(single),
        (((1,), (1,)), ((), ())),
        precision=lax.Precision.HIGHEST,
        preferred_element_type=single,
    )
    small = reduce_small(
        jnp.concatenate([norm_terms.reshape(-1), grad_head0, grad_head1]).reshape(-1, 128)
    ).reshape(-1)
    norm_wgrad = small[: 4 * width].reshape(4, width)
    head_wgrad = small[4 * width :].reshape(2, HEAD)

    query_set = adam_update(query_weight, query_first, query_second, attn_owned[0])
    keyval_set = adam_update(
        keyval_weight,
        keyval_first,
        keyval_second,
        jnp.stack([keyval_owned[:, :slice_len], keyval_owned[:, slice_len:]]),
    )
    output_set = adam_update(output_weight, output_first, output_second, attn_owned[1].T)
    gateup_set = adam_update(
        gateup_weight, gateup_first, gateup_second, ffn_owned[:2]
    )
    down_set = adam_update(down_weight, down_first, down_second, ffn_owned[2].T)
    norm_set = adam_update(norm_scales, norm_first, norm_second, norm_wgrad)
    head_set = adam_update(head_scales, head_first, head_second, head_wgrad)
    return (
        (block_out, tokens_grad)
        + query_set
        + keyval_set
        + output_set
        + gateup_set
        + down_set
        + norm_set
        + head_set
    )


def solution(mesh):
    placed = (
        P(("ctx", "shard"), None),
        P(),
        P(("ctx", "shard"), None),
        P("ctx", "shard"),
        P("ctx", "shard"),
        P("ctx", "shard"),
        P(None, "ctx", "shard"),
        P(None, "ctx", "shard"),
        P(None, "ctx", "shard"),
        P("shard", "ctx"),
        P("shard", "ctx"),
        P("shard", "ctx"),
        P(None, "ctx", "shard"),
        P(None, "ctx", "shard"),
        P(None, "ctx", "shard"),
        P("shard", "ctx"),
        P("shard", "ctx"),
        P("shard", "ctx"),
        P(),
        P(),
        P(),
        P(),
        P(),
        P(),
    )
    return jax.shard_map(
        shards,
        mesh=mesh,
        in_specs=placed,
        out_specs=(
            P(("ctx", "shard"), None),
            P(("ctx", "shard"), None),
            P("ctx", "shard"),
            P("ctx", "shard"),
            P("ctx", "shard"),
            P("ctx", "shard"),
            P(None, "ctx", "shard"),
            P(None, "ctx", "shard"),
            P(None, "ctx", "shard"),
            P(None, "ctx", "shard"),
            P("shard", "ctx"),
            P("shard", "ctx"),
            P("shard", "ctx"),
            P("shard", "ctx"),
            P(None, "ctx", "shard"),
            P(None, "ctx", "shard"),
            P(None, "ctx", "shard"),
            P(None, "ctx", "shard"),
            P("shard", "ctx"),
            P("shard", "ctx"),
            P("shard", "ctx"),
            P("shard", "ctx"),
            P(),
            P(),
            P(),
            P(),
            P(),
            P(),
            P(),
            P(),
        ),
        check_vma=False,
    )
```

```python
import jax
import jax.numpy as jnp
from jax import lax
from jax.experimental import pallas as pl
from jax.experimental.pallas import tpu as pltpu
from jax.sharding import PartitionSpec as P

HEADS = 4
HEAD = 256
STEP = 3


norm_eps = 1e-06
rope_base = 1000000.0
score_scale = 0.0625
learn_rate = 0.02
beta_first = 0.9
beta_second = 0.95
adam_eps = 1e-08
weight_decay = 0.1
gelu_coef = 0.7978845608028654
masked_value = -1e30


def rms_forward(values):
    inverse = lax.rsqrt(jnp.mean(values * values, axis=-1, keepdims=True) + norm_eps)
    return (values * inverse, inverse)


def rms_backward(normed, inverse, upstream):
    return inverse * (upstream - normed * jnp.mean(upstream * normed, axis=-1, keepdims=True))


def rotate(values):
    middle = values.shape[-1] // 2
    return jnp.concatenate([-values[..., middle:], values[..., :middle]], axis=-1)


def rotate_back(values):
    middle = values.shape[-1] // 2
    return jnp.concatenate([values[..., middle:], -values[..., :middle]], axis=-1)


def rope_tables(places):
    middle = HEAD // 2
    freqs = rope_base ** (-(jnp.arange(middle, dtype=jnp.float32) * 2.0 / HEAD))
    angles = places.astype(jnp.float32)[:, None] * freqs[None, :]
    cosine = jnp.cos(angles)
    sine = jnp.sin(angles)
    return (jnp.concatenate([cosine, cosine], axis=-1), jnp.concatenate([sine, sine], axis=-1))


def gelu_parts(values):
    inner = gelu_coef * (values + 0.044715 * values * values * values)
    tangent = jnp.tanh(inner)
    result = 0.5 * values * (1.0 + tangent)
    slope = 0.5 * (1.0 + tangent) + 0.5 * values * (1.0 - tangent * tangent) * gelu_coef * (
        1.0 + 3.0 * 0.044715 * values * values
    )
    return (result, slope)


def adam_update(weight, first, second, grad):
    first_new = beta_first * first + (1.0 - beta_first) * grad
    second_new = beta_second * second + (1.0 - beta_second) * grad * grad
    first_hat = first_new / (1.0 - beta_first**STEP)
    second_hat = second_new / (1.0 - beta_second**STEP)
    weight_new = weight - learn_rate * (
        first_hat / (jnp.sqrt(second_hat) + adam_eps) + weight_decay * weight
    )
    return (grad, weight_new, first_new, second_new)


def swap(piece, axis, distance):
    return lax.ppermute(piece, axis, [(i, i ^ distance) for i in range(lax.axis_size(axis))])


def chip_count():
    return lax.axis_size("ctx") // 2


def after(value, marks):
    return lax.optimization_barrier((value, marks))[0]


def gather_shard(piece, dim):
    got = [swap(piece, "shard", j) for j in range(1, lax.axis_size("shard"))]
    return (jnp.concatenate([piece] + got, axis=dim), got)


def gather_pair(piece, dim):
    return jnp.concatenate([piece, swap(piece, "shard", 1)], axis=dim)


def scatter_pair(terms):
    keep, send = jnp.split(terms, 2, axis=0)
    return keep + swap(send.astype(jnp.bfloat16), "shard", 1).astype(jnp.float32)


def gather_cores(piece, dim):
    return jnp.concatenate([piece, swap(piece, "ctx", 1)], axis=dim)


def tree_sum(terms):
    while len(terms) > 1:
        terms = [terms[i] + terms[i + 1] for i in range(0, len(terms), 2)]
    return terms[0]


def wide_sum(terms):
    return tree_sum([piece.astype(jnp.float32) for piece in terms])


def scatter_cores(terms, dim):
    keep = lax.index_in_dim(terms, 0, dim, keepdims=False)
    send = lax.index_in_dim(terms, 1, dim, keepdims=False)
    return wide_sum([keep, swap(send, "ctx", 1)])


def scatter_chips(terms, dim):
    parts = jnp.split(terms, chip_count(), axis=dim)
    got = [swap(parts[k], "ctx", 2 * k) for k in range(1, len(parts))]
    return (wide_sum([parts[0]] + got), got)


def scatter_shard(terms, dim):
    parts = jnp.split(terms, lax.axis_size("shard"), axis=dim)
    return wide_sum([parts[0]] + [swap(parts[j], "shard", j) for j in range(1, len(parts))])


def gather_rows(piece, begin, end):
    piece = after(piece, begin)
    marks = [swap(piece, "ctx", 2 * k) for k in range(1, chip_count())]
    rows = jnp.concatenate(after([piece] + marks, end), axis=-2)
    split = rows.reshape(rows.shape[:-2] + (chip_count(), 1, piece.shape[-2], rows.shape[-1]))
    whole = gather_cores(split, -3).reshape(
        rows.shape[:-2] + (2 * rows.shape[-2], rows.shape[-1])
    )
    return (whole, marks)


def core_rows(rows):
    split = rows.reshape(rows.shape[:-2] + (chip_count(), 1, -1, rows.shape[-1]))
    return gather_cores(split, -3).reshape(
        rows.shape[:-2] + (2 * rows.shape[-2], rows.shape[-1])
    )


def scatter_rows(terms, begin):
    chips = chip_count()
    rows = terms.shape[-2] // (2 * chips)
    split = terms.reshape(terms.shape[:-2] + (chips, 2, rows, terms.shape[-1]))
    summed = scatter_cores(split, split.ndim - 3).astype(jnp.bfloat16)
    summed = summed.reshape(terms.shape[:-2] + (chips * rows, terms.shape[-1]))
    return scatter_chips(after(summed, begin), -2)


def split_wide(values):
    high = lax.reduce_precision(values, 8, 7)
    low = lax.reduce_precision(values - high, 8, 7)
    return (high + low, jnp.concatenate([high, low], axis=0).astype(jnp.bfloat16))


def join_wide(packed, shape):
    high, low = jnp.split(packed.reshape((2,) + shape).astype(jnp.float32), 2, axis=0)
    return (high + low)[0]


def scatter_last(terms, small, attn_terms):
    chips = chip_count()
    shards_n = lax.axis_size("shard")
    rows = terms.shape[0] // (2 * chips)
    shape = small.shape
    split = terms.reshape(chips, 2, rows, terms.shape[1])
    summed = scatter_cores(split, 1).astype(jnp.bfloat16)
    small = small + swap(small, "ctx", 1)
    own, packed = split_wide(small)
    packed = packed.reshape(-1, terms.shape[1])
    got = [
        swap(jnp.concatenate([summed[k], packed], axis=0), "ctx", 2 * k)
        for k in range(1, chips)
    ]
    small = tree_sum([own] + [join_wide(piece[rows:], shape) for piece in got])
    summed = wide_sum([summed[0]] + [piece[:rows] for piece in got]).astype(jnp.bfloat16)
    own, packed = split_wide(small)
    attn_parts = jnp.split(attn_terms.astype(jnp.bfloat16), shards_n, axis=-1)
    parts = jnp.split(summed, shards_n, axis=1)
    width = attn_parts[0].shape[-1]

    def flat(value):
        return value.reshape(-1, width)

    def message(j):
        return jnp.concatenate([flat(packed), flat(attn_parts[j]), flat(parts[j])], axis=0)

    mine = message(0)
    got = [swap(message(j), "shard", j) for j in range(1, shards_n)]
    small_rows = packed.size // width
    attn_rows = small_rows + attn_parts[0].size // width
    term_rows = attn_rows + parts[0].size // width
    small = tree_sum([own] + [join_wide(piece[:small_rows], shape) for piece in got])
    total = wide_sum([mine[small_rows:term_rows]] + [piece[small_rows:term_rows] for piece in got])
    return (
        total[: attn_rows - small_rows].reshape(attn_parts[0].shape),
        total[attn_rows - small_rows :].reshape(parts[0].shape),
        small,
    )


def relative_ctx(index):
    return lax.axis_index("ctx") ^ index


def one_hot(source):
    size = source.shape[0]
    return (jnp.arange(size, dtype=jnp.int32)[:, None] == source[None, :]).astype(jnp.bfloat16)


def nn(left, right):
    return jnp.dot(left, right, preferred_element_type=jnp.float32)


def nt(left, right):
    return lax.dot_general(
        left, right, (((1,), (1,)), ((), ())), preferred_element_type=jnp.float32
    )


def tn(left, right):
    return lax.dot_general(
        left, right, (((0,), (0,)), ((), ())), preferred_element_type=jnp.float32
    )


def stack_heads(rows, half_len):
    return jnp.concatenate(
        [
            rows[side * half_len : (side + 1) * half_len, h * HEAD : (h + 1) * HEAD]
            for side in range(2)
            for h in range(HEADS)
        ],
        axis=0,
    )


def key_block(kv_ref, table_ref, block_index, shard_size, part):
    half_blocks = table_ref.shape[0] - 2
    high = (block_index >= half_blocks).astype(jnp.int32)
    at = table_ref[jnp.where(high == 1, 2 * half_blocks - 1 - block_index, block_index)]
    piece = kv_ref[at, :, high, :, part * HEAD : (part + 1) * HEAD]
    return piece.reshape(piece.shape[0] * piece.shape[1], HEAD)


def start_keys(piece_refs, kv_ref, sem_ref):
    copies = [
        pltpu.make_async_copy(piece_ref, kv_ref.at[i], sem_ref.at[i])
        for i, piece_ref in enumerate(piece_refs)
    ]
    for copy in copies:
        copy.start()
    return copies


def forward_kernel(table_ref, query_ref, *refs):
    half_blocks = table_ref.shape[0] - 2
    piece_refs = refs[:half_blocks]
    out_ref, log_ref, q_s, acc_s, sum_s, kv_ref, sem_ref = refs[half_blocks:]
    copies = start_keys(piece_refs, kv_ref, sem_ref)
    shard_size = kv_ref.shape[1]
    half_len = kv_ref.shape[3]
    block_len = shard_size * half_len
    side_rows = half_len * HEADS
    own_block = table_ref[half_blocks]
    own_shard = table_ref[half_blocks + 1]
    far_block = 2 * half_blocks - 1 - own_block
    q_s[...] = stack_heads(query_ref[...], half_len)
    acc_s[...] = jnp.zeros_like(acc_s)
    sum_s[...] = jnp.zeros_like(sum_s)
    key_i = lax.broadcasted_iota(jnp.int32, (1, block_len), 1)
    key_in = ((key_i // half_len) ^ own_shard) * half_len + key_i % half_len
    row_i = lax.broadcasted_iota(jnp.int32, (side_rows, 1), 0)
    query_in = own_shard * half_len + row_i % half_len
    offset_in = key_in - query_in
    for copy in copies:
        copy.wait()

    def attend(unit):
        far = (unit > own_block).astype(jnp.int32)
        block_index = unit - far * (own_block + 1)
        query_block = jnp.where(far == 1, far_block, own_block)
        rows = pl.ds(pl.multiple_of(far * side_rows, side_rows), side_rows)
        keys = key_block(kv_ref, table_ref, block_index, shard_size, 0)
        values = key_block(kv_ref, table_ref, block_index, shard_size, 1)
        scores = nt(q_s[rows, :], keys) * score_scale
        visible = offset_in <= (query_block - block_index) * block_len
        weights = jnp.where(visible, jnp.exp(scores), 0.0)
        return (
            rows,
            jnp.sum(weights, axis=-1, keepdims=True),
            nn(weights.astype(jnp.bfloat16), values),
        )

    def attend_some(first, count):
        for rows, total, mixed in [attend(first + i) for i in range(count)]:
            sum_s[rows, :] += total
            acc_s[rows, :] += mixed

    unit_count = 2 * half_blocks + 1
    group = 4

    def attend_group(index, carry):
        attend_some(index * group, group)
        return carry

    lax.fori_loop(0, unit_count // group, attend_group, 0)
    attend_some(unit_count - unit_count % group, unit_count % group)
    total = sum_s[...]
    result = acc_s[...] / total
    log_ref[...] = jnp.log(total)
    for side in range(2):
        for h in range(HEADS):
            at = (side * HEADS + h) * half_len
            out_ref[side * half_len : (side + 1) * half_len, h * HEAD : (h + 1) * HEAD] = result[
                at : at + half_len, :
            ]


def backward_kernel(
    table_ref, query_ref, out_ref, grad_ref, log_ref, *refs
):
    half_blocks = table_ref.shape[0] - 2
    piece_refs = refs[:half_blocks]
    dq_ref, keep_ref, send_ref = refs[half_blocks : half_blocks + 3]
    q_s, do_s, acc_s, log_s, delta_s, kv_ref, dkv_ref, sem_ref = refs[half_blocks + 3 :]
    copies = start_keys(piece_refs, kv_ref, sem_ref)
    shard_size = kv_ref.shape[1]
    half_len = kv_ref.shape[3]
    block_len = shard_size * half_len
    side_rows = half_len * HEADS
    own_block = table_ref[half_blocks]
    own_shard = table_ref[half_blocks + 1]
    far_block = 2 * half_blocks - 1 - own_block
    q_s[...] = stack_heads(query_ref[...], half_len)
    grads = stack_heads(grad_ref[...], half_len)
    do_s[...] = grads
    outs = stack_heads(out_ref[...], half_len)
    delta_all = jnp.transpose(
        jnp.sum(grads.astype(jnp.float32) * outs, axis=-1, keepdims=True)
    )
    log_all = jnp.transpose(log_ref[...])
    acc_s[...] = jnp.zeros_like(acc_s)
    shape = (shard_size, half_len, HEAD)
    for side in range(2):
        log_s[side] = log_all[:, side * side_rows : (side + 1) * side_rows]
        delta_s[side] = delta_all[:, side * side_rows : (side + 1) * side_rows]
    key_i = lax.broadcasted_iota(jnp.int32, (block_len, 1), 0)
    key_in = ((key_i // half_len) ^ own_shard) * half_len + key_i % half_len
    row_i = lax.broadcasted_iota(jnp.int32, (1, side_rows), 1)
    query_in = own_shard * half_len + row_i % half_len
    offset_in = key_in - query_in
    for copy in copies:
        copy.wait()

    def attend(unit):
        far = (unit > own_block).astype(jnp.int32)
        block_index = unit - far * (own_block + 1)
        query_block = jnp.where(far == 1, far_block, own_block)
        rows = pl.ds(pl.multiple_of(far * side_rows, side_rows), side_rows)
        high = (block_index >= half_blocks).astype(jnp.int32)
        at = table_ref[jnp.where(high == 1, 2 * half_blocks - 1 - block_index, block_index)]
        keys = key_block(kv_ref, table_ref, block_index, shard_size, 0)
        values = key_block(kv_ref, table_ref, block_index, shard_size, 1)
        queries = q_s[rows, :]
        grad_rows = do_s[rows, :]
        scores = nt(keys, queries) * score_scale
        visible = offset_in <= (query_block - block_index) * block_len
        weights = jnp.where(visible, jnp.exp(scores - log_s[far]), 0.0)
        grad_weights = nt(values, grad_rows)
        grad_scores = (weights * (grad_weights - delta_s[far])).astype(jnp.bfloat16)
        dq = tn(grad_scores, keys)
        dk = nn(grad_scores, queries) * score_scale
        dv = nn(weights.astype(jnp.bfloat16), grad_rows)
        seen = jnp.logical_and(far == 1, block_index <= own_block)
        return (rows, (at % 2, at // 2), high, seen, dq, dk, dv)

    def attend_some(first, count):
        for rows, (core, chip), high, seen, dq, dk, dv in [attend(first + i) for i in range(count)]:
            acc_s[rows, :] += dq
            for part, value in enumerate((dk, dv)):
                columns = slice(part * HEAD, (part + 1) * HEAD)
                old = dkv_ref[core, chip, :, high, :, columns].astype(jnp.float32)
                dkv_ref[core, chip, :, high, :, columns] = (
                    value.reshape(shape) + jnp.where(seen, old, 0.0)
                ).astype(jnp.bfloat16)

    def none(block_index, carry):
        at = table_ref[2 * half_blocks - 1 - block_index]
        dkv_ref[at % 2, at // 2, :, 1] = jnp.zeros(
            (shard_size, half_len, 2 * HEAD), jnp.bfloat16
        )
        return carry

    unit_count = 2 * half_blocks + 1
    group = 4

    def attend_group(index, carry):
        attend_some(index * group, group)
        return carry

    lax.fori_loop(0, unit_count // group, attend_group, 0)
    attend_some(unit_count - unit_count % group, unit_count % group)
    lax.fori_loop(far_block + 1, 2 * half_blocks, none, 0)
    copies = [
        pltpu.make_async_copy(dkv_ref.at[i], target_ref, sem_ref.at[i])
        for i, target_ref in enumerate((keep_ref, send_ref))
    ]
    for copy in copies:
        copy.start()
    result = acc_s[...] * score_scale
    for side in range(2):
        for h in range(HEADS):
            at = (side * HEADS + h) * half_len
            dq_ref[side * half_len : (side + 1) * half_len, h * HEAD : (h + 1) * HEAD] = result[
                at : at + half_len, :
            ]
    for copy in copies:
        copy.wait()


def whole_spec(space=pltpu.VMEM):
    return pl.BlockSpec(memory_space=space)


def attention_forward(table, queries, pieces):
    rows = queries.shape[0] * HEADS
    kv_size = len(pieces) * pieces[0].size
    return pl.pallas_call(
        forward_kernel,
        out_shape=(
            jax.ShapeDtypeStruct(queries.shape, jnp.float32),
            jax.ShapeDtypeStruct((rows, 1), jnp.float32),
        ),
        in_specs=[whole_spec(pltpu.SMEM), whole_spec()] + [whole_spec(pl.ANY)] * len(pieces),
        out_specs=(whole_spec(), whole_spec()),
        scratch_shapes=[
            pltpu.VMEM((rows, HEAD), jnp.bfloat16),
            pltpu.VMEM((rows, HEAD), jnp.float32),
            pltpu.VMEM((rows, 1), jnp.float32),
            pltpu.VMEM((len(pieces),) + pieces[0].shape, jnp.bfloat16),
            pltpu.SemaphoreType.DMA((len(pieces),)),
        ],
        compiler_params=pltpu.CompilerParams(vmem_limit_bytes=2 * kv_size + (24 << 20)),
        name="attention_forward",
    )(table, queries, *pieces)


def attention_backward(table, queries, pieces, outs, grads, logs):
    rows = queries.shape[0] * HEADS
    kv_size = len(pieces) * pieces[0].size
    half = (len(pieces) // 2,) + pieces[0].shape
    return pl.pallas_call(
        backward_kernel,
        out_shape=(
            jax.ShapeDtypeStruct(queries.shape, jnp.float32),
            jax.ShapeDtypeStruct(half, jnp.bfloat16),
            jax.ShapeDtypeStruct(half, jnp.bfloat16),
        ),
        in_specs=[whole_spec(pltpu.SMEM)]
        + [whole_spec()] * 4
        + [whole_spec(pl.ANY)] * len(pieces),
        out_specs=(whole_spec(), whole_spec(pl.ANY), whole_spec(pl.ANY)),
        scratch_shapes=[
            pltpu.VMEM((rows, HEAD), jnp.bfloat16),
            pltpu.VMEM((rows, HEAD), jnp.bfloat16),
            pltpu.VMEM((rows, HEAD), jnp.float32),
            pltpu.VMEM((2, 1, rows // 2), jnp.float32),
            pltpu.VMEM((2, 1, rows // 2), jnp.float32),
            pltpu.VMEM((len(pieces),) + pieces[0].shape, jnp.bfloat16),
            pltpu.VMEM((2,) + half, jnp.bfloat16),
            pltpu.SemaphoreType.DMA((len(pieces),)),
        ],
        compiler_params=pltpu.CompilerParams(vmem_limit_bytes=4 * kv_size + (24 << 20)),
        name="attention_backward",
    )(table, queries, outs, grads, logs, *pieces)


def shards(
    tokens,
    positions,
    cotangent,
    query_weight,
    query_first,
    query_second,
    keyval_weight,
    keyval_first,
    keyval_second,
    output_weight,
    output_first,
    output_second,
    gateup_weight,
    gateup_first,
    gateup_second,
    down_weight,
    down_first,
    down_second,
    norm_scales,
    norm_first,
    norm_second,
    head_scales,
    head_first,
    head_second,
):
    bfloat = jnp.bfloat16
    single = jnp.float32
    ctx_size = lax.axis_size("ctx")
    shard_size = lax.axis_size("shard")
    ctx_at = lax.axis_index("ctx")
    shard_at = lax.axis_index("shard")
    row_count, width = tokens.shape
    half_len = row_count // 2
    block_len = half_len * shard_size
    piece_len = width // ctx_size
    slice_len = HEAD // shard_size

    group_tokens, token_marks = gather_shard(tokens, 0)
    attn_pieces, _ = gather_shard(
        jnp.concatenate(
            [
                keyval_weight[0].astype(bfloat),
                keyval_weight[1].astype(bfloat),
                query_weight.astype(bfloat),
                output_weight.astype(bfloat).T,
            ],
            axis=-1,
        )[None],
        0,
    )
    ffn_piece = after(
        jnp.stack(
            [
                gateup_weight[0].astype(bfloat),
                gateup_weight[1].astype(bfloat),
                down_weight.astype(bfloat).T,
            ]
        ),
        token_marks,
    )
    ffn_z = jnp.concatenate(
        [ffn_piece] + [swap(ffn_piece, "shard", j) for j in range(2, shard_size, 2)], axis=-1
    )

    def side_by_side(start, size):
        return jnp.concatenate(
            [attn_pieces[j, :, start : start + size] for j in range(shard_size)], axis=-1
        )

    keyval_full, keyval_marks = gather_rows(side_by_side(0, 2 * slice_len), [], [])

    feature = jnp.arange(width, dtype=jnp.int32)
    feature_map = one_hot(relative_ctx(feature // piece_len) * piece_len + feature % piece_len)
    channel = jnp.arange(2 * HEAD, dtype=jnp.int32)
    channel_map = one_hot(
        ((channel % HEAD) // slice_len ^ shard_at) * (2 * slice_len)
        + (channel // HEAD) * slice_len
        + channel % slice_len
    )
    keyval_sorted = nn(keyval_full, channel_map).astype(bfloat)

    scales = lax.dot_general(
        norm_scales,
        feature_map.astype(single),
        (((1,), (0,)), ((), ())),
        precision=lax.Precision.HIGHEST,
        preferred_element_type=single,
    )
    group_inputs = nn(group_tokens, feature_map)
    inputs = group_inputs[:row_count]
    upstream = nn(cotangent, feature_map)

    ctx_places = lax.dynamic_slice_in_dim(
        positions, ctx_at * shard_size * row_count, shard_size * row_count
    ).reshape(shard_size, row_count)
    piece = jnp.arange(shard_size, dtype=jnp.int32)
    group_at = jnp.sum(
        jnp.where(
            ((piece ^ shard_at)[:, None] == piece[None, :])[:, :, None], ctx_places[None], 0
        ),
        axis=1,
    ).reshape(-1)
    first_at = positions.reshape(ctx_size, shard_size * row_count)[:, 0] // block_len
    rel = jnp.arange(ctx_size, dtype=jnp.int32)
    blocks_rel = jnp.sum(
        jnp.where(relative_ctx(rel)[:, None] == rel[None, :], first_at[None, :], 0), axis=1
    )
    places = jnp.sum(
        jnp.where(blocks_rel[None, :] == rel[:, None], rel[None, :], 0), axis=1
    )
    table = jnp.concatenate(
        [places, blocks_rel[:1], jnp.full((1,), shard_at, jnp.int32)]
    ).astype(jnp.int32)

    group_normed, group_inverse = rms_forward(group_inputs)
    group_in = (group_normed * (1.0 + scales[0])).astype(bfloat)
    normed_in, inverse_in = (group_normed[:row_count], group_inverse[:row_count])
    attn_in = group_in[:row_count]
    group_cosine, group_sine = rope_tables(group_at)
    cosine, sine = (group_cosine[:row_count], group_sine[:row_count])
    keyval_proj = nn(group_in, keyval_sorted)
    group_key_normed, group_key_inverse = rms_forward(keyval_proj[:, :HEAD])
    key_normed, key_inverse = (group_key_normed[:row_count], group_key_inverse[:row_count])
    key_scaled = group_key_normed * (1.0 + head_scales[1])
    keys_own = (key_scaled * group_cosine + rotate(key_scaled) * group_sine).astype(bfloat)
    values_own = keyval_proj[:, HEAD:].astype(bfloat)
    kv_own = jnp.concatenate([keys_own, values_own], axis=-1).reshape(
        shard_size, 2, half_len, 2 * HEAD
    )
    attn_own = after(
        jnp.stack([side_by_side(2 * slice_len, HEAD), side_by_side(2 * slice_len + HEAD, HEAD)]),
        keyval_marks,
    )
    attn_got = [attn_own] + [swap(attn_own, "ctx", 2 * k) for k in range(1, chip_count())]
    kv_marks = [swap(kv_own, "ctx", 2 * k) for k in range(1, chip_count())]
    attn_got = after(attn_got, (kv_marks, ffn_z))
    attn_full = core_rows(jnp.concatenate(attn_got, axis=-2))
    query_full, output_full = (attn_full[0], attn_full[1])
    query_proj = nn(attn_in, query_full)
    query_normed, query_inverse = rms_forward(query_proj.reshape(row_count, HEADS, HEAD))
    query_scaled = query_normed * (1.0 + head_scales[0])
    query_rows = (
        (query_scaled * cosine[:, None, :] + rotate(query_scaled) * sine[:, None, :])
        .astype(bfloat)
        .reshape(row_count, HEADS * HEAD)
    )
    kv_pieces = [
        piece
        for own in [kv_own] + kv_marks
        for piece in (own, swap(own, "ctx", 1))
    ]

    attn_rows, attn_logs = attention_forward(table, query_rows, kv_pieces)
    ffn_full, _ = gather_rows(ffn_z, kv_marks, attn_rows)
    gate_full, up_full, down_full = (ffn_full[0], ffn_full[1], ffn_full[2])
    attn_b = attn_rows.astype(bfloat)
    attn_out = nt(attn_b, output_full)
    out_normed, out_inverse = rms_forward(attn_out)
    hidden_in = inputs + out_normed * (1.0 + scales[1])
    mid_normed, mid_inverse = rms_forward(hidden_in)
    ffn_in = (mid_normed * (1.0 + scales[2])).astype(bfloat)
    group_ffn = gather_pair(ffn_in, 0)
    gate_pre = nn(group_ffn, gate_full)
    up_pre = nn(group_ffn, up_full)
    gate_value, gate_slope = gelu_parts(gate_pre)
    hidden_b = (gate_value * up_pre).astype(bfloat)
    ffn_out = scatter_pair(nt(hidden_b, down_full))
    ffn_normed, ffn_inverse = rms_forward(ffn_out)
    block_out = nt(
        (hidden_in + ffn_normed * (1.0 + scales[3])).astype(bfloat), feature_map
    ).astype(bfloat)
    grad_norm3 = jnp.sum(upstream * ffn_normed, axis=0)
    ffn_grad = rms_backward(ffn_normed, ffn_inverse, upstream * (1.0 + scales[3])).astype(bfloat)
    group_grad = gather_pair(ffn_grad, 0)
    hidden_grad = nn(group_grad, down_full)
    gate_grad = (hidden_grad * up_pre * gate_slope).astype(bfloat)
    up_grad = (hidden_grad * gate_value).astype(bfloat)
    ffn_in_grad = scatter_pair(nt(gate_grad, gate_full) + nt(up_grad, up_full))
    ffn_rows, ffn_marks = scatter_rows(
        jnp.stack(
            [
                tn(group_ffn, gate_grad).astype(bfloat),
                tn(group_ffn, up_grad).astype(bfloat),
                tn(group_grad, hidden_b).astype(bfloat),
            ]
        ),
        [],
    )
    ffn_parts = jnp.split(ffn_rows.astype(bfloat), shard_size // 2, axis=-1)
    ffn_owned = wide_sum(
        [ffn_parts[0]] + [swap(ffn_parts[j], "shard", 2 * j) for j in range(1, len(ffn_parts))]
    )
    grad_norm2 = jnp.sum(ffn_in_grad * mid_normed, axis=0)
    residual_grad = upstream + rms_backward(mid_normed, mid_inverse, ffn_in_grad * (1.0 + scales[2]))
    grad_norm1 = jnp.sum(residual_grad * out_normed, axis=0)
    attn_out_grad = rms_backward(
        out_normed, out_inverse, residual_grad * (1.0 + scales[1])
    ).astype(bfloat)
    attn_grad_b = nn(attn_out_grad, output_full).astype(bfloat)
    query_parts, kv_keep, kv_send = attention_backward(
        table, query_rows, kv_pieces, attn_rows, attn_grad_b, attn_logs
    )
    kv_keep, kv_send = after((kv_keep, kv_send), ffn_marks)
    kv_terms = wide_sum([kv_keep, swap(kv_send, "ctx", 1)]).astype(bfloat)
    kv_core = kv_terms
    kv_terms, kv_marks = scatter_chips(kv_terms, 0)
    kv_grad = scatter_shard(kv_terms.astype(bfloat)[0], 0).reshape(row_count, 2 * HEAD)
    query_rot_grad = query_parts.reshape(row_count, HEADS, HEAD)
    query_rope_grad = query_rot_grad * cosine[:, None, :] + rotate_back(
        query_rot_grad * sine[:, None, :]
    )
    grad_head0 = jnp.sum(query_rope_grad * query_normed, axis=(0, 1))
    query_proj_grad = (
        rms_backward(query_normed, query_inverse, query_rope_grad * (1.0 + head_scales[0]))
        .reshape(row_count, HEADS * HEAD)
        .astype(bfloat)
    )
    late_grad, late_out_grad = after((query_proj_grad, attn_out_grad), kv_core)
    query_wgrad = tn(attn_in, late_grad).astype(bfloat)
    output_wgrad = tn(late_out_grad, attn_b).astype(bfloat)
    attn_terms, attn_marks = scatter_rows(jnp.stack([query_wgrad, output_wgrad]), kv_marks)
    kv_grad = after(kv_grad, attn_marks)
    key_rot_grad = kv_grad[:, :HEAD]
    value_grad = kv_grad[:, HEAD:]
    key_rope_grad = key_rot_grad * cosine + rotate_back(key_rot_grad * sine)
    grad_head1 = jnp.sum(key_rope_grad * key_normed, axis=0)
    key_proj_grad = rms_backward(
        key_normed, key_inverse, key_rope_grad * (1.0 + head_scales[1])
    ).astype(bfloat)
    keyval_proj_grad = jnp.concatenate([key_proj_grad, value_grad.astype(bfloat)], axis=-1)
    keyval_wgrad = nt(tn(attn_in, keyval_proj_grad).astype(bfloat), channel_map).astype(bfloat)
    attn_in_grad = nt(query_proj_grad, query_full) + nt(keyval_proj_grad, keyval_sorted)
    grad_norm0 = jnp.sum(attn_in_grad * normed_in, axis=0)
    tokens_grad = nt(
        (
            residual_grad
            + rms_backward(normed_in, inverse_in, attn_in_grad * (1.0 + scales[0]))
        ).astype(bfloat),
        feature_map,
    ).astype(bfloat)
    norm_terms = lax.dot_general(
        jnp.stack([grad_norm0, grad_norm1, grad_norm2, grad_norm3]),
        feature_map.astype(single),
        (((1,), (1,)), ((), ())),
        precision=lax.Precision.HIGHEST,
        preferred_element_type=single,
    )
    attn_owned, keyval_owned, small = scatter_last(
        keyval_wgrad,
        jnp.concatenate([norm_terms.reshape(-1), grad_head0, grad_head1]).reshape(-1, 128),
        attn_terms,
    )
    small = small.reshape(-1)
    norm_wgrad = small[: 4 * width].reshape(4, width)
    head_wgrad = small[4 * width :].reshape(2, HEAD)

    query_set = adam_update(query_weight, query_first, query_second, attn_owned[0])
    keyval_set = adam_update(
        keyval_weight,
        keyval_first,
        keyval_second,
        jnp.stack([keyval_owned[:, :slice_len], keyval_owned[:, slice_len:]]),
    )
    output_set = adam_update(output_weight, output_first, output_second, attn_owned[1].T)
    gateup_set = adam_update(
        gateup_weight, gateup_first, gateup_second, ffn_owned[:2]
    )
    down_set = adam_update(down_weight, down_first, down_second, ffn_owned[2].T)
    norm_set = adam_update(norm_scales, norm_first, norm_second, norm_wgrad)
    head_set = adam_update(head_scales, head_first, head_second, head_wgrad)
    return (
        (block_out, tokens_grad)
        + query_set
        + keyval_set
        + output_set
        + gateup_set
        + down_set
        + norm_set
        + head_set
    )


def solution(mesh):
    placed = (
        P(("ctx", "shard"), None),
        P(),
        P(("ctx", "shard"), None),
        P("ctx", "shard"),
        P("ctx", "shard"),
        P("ctx", "shard"),
        P(None, "ctx", "shard"),
        P(None, "ctx", "shard"),
        P(None, "ctx", "shard"),
        P("shard", "ctx"),
        P("shard", "ctx"),
        P("shard", "ctx"),
        P(None, "ctx", "shard"),
        P(None, "ctx", "shard"),
        P(None, "ctx", "shard"),
        P("shard", "ctx"),
        P("shard", "ctx"),
        P("shard", "ctx"),
        P(),
        P(),
        P(),
        P(),
        P(),
        P(),
    )
    return jax.shard_map(
        shards,
        mesh=mesh,
        in_specs=placed,
        out_specs=(
            P(("ctx", "shard"), None),
            P(("ctx", "shard"), None),
            P("ctx", "shard"),
            P("ctx", "shard"),
            P("ctx", "shard"),
            P("ctx", "shard"),
            P(None, "ctx", "shard"),
            P(None, "ctx", "shard"),
            P(None, "ctx", "shard"),
            P(None, "ctx", "shard"),
            P("shard", "ctx"),
            P("shard", "ctx"),
            P("shard", "ctx"),
            P("shard", "ctx"),
            P(None, "ctx", "shard"),
            P(None, "ctx", "shard"),
            P(None, "ctx", "shard"),
            P(None, "ctx", "shard"),
            P("shard", "ctx"),
            P("shard", "ctx"),
            P("shard", "ctx"),
            P("shard", "ctx"),
            P(),
            P(),
            P(),
            P(),
            P(),
            P(),
            P(),
            P(),
        ),
        check_vma=False,
    )
```

```python
import jax
import jax.numpy as jnp
from jax import lax
from jax.experimental import pallas as pl
from jax.experimental.pallas import tpu as pltpu
from jax.sharding import PartitionSpec as P

HEADS = 4
HEAD = 256
STEP = 3


norm_eps = 1e-06
rope_base = 1000000.0
score_scale = 0.0625
learn_rate = 0.02
beta_first = 0.9
beta_second = 0.95
adam_eps = 1e-08
weight_decay = 0.1
gelu_coef = 0.7978845608028654
masked_value = -1e30


def rms_forward(values):
    inverse = lax.rsqrt(jnp.mean(values * values, axis=-1, keepdims=True) + norm_eps)
    return (values * inverse, inverse)


def rms_backward(normed, inverse, upstream):
    return inverse * (upstream - normed * jnp.mean(upstream * normed, axis=-1, keepdims=True))


def rotate(values):
    middle = values.shape[-1] // 2
    return jnp.concatenate([-values[..., middle:], values[..., :middle]], axis=-1)


def rotate_back(values):
    middle = values.shape[-1] // 2
    return jnp.concatenate([values[..., middle:], -values[..., :middle]], axis=-1)


def rope_tables(places):
    middle = HEAD // 2
    freqs = rope_base ** (-(jnp.arange(middle, dtype=jnp.float32) * 2.0 / HEAD))
    angles = places.astype(jnp.float32)[:, None] * freqs[None, :]
    cosine = jnp.cos(angles)
    sine = jnp.sin(angles)
    return (jnp.concatenate([cosine, cosine], axis=-1), jnp.concatenate([sine, sine], axis=-1))


def gelu_parts(values):
    inner = gelu_coef * (values + 0.044715 * values * values * values)
    tangent = jnp.tanh(inner)
    result = 0.5 * values * (1.0 + tangent)
    slope = 0.5 * (1.0 + tangent) + 0.5 * values * (1.0 - tangent * tangent) * gelu_coef * (
        1.0 + 3.0 * 0.044715 * values * values
    )
    return (result, slope)


def adam_update(weight, first, second, grad):
    first_new = beta_first * first + (1.0 - beta_first) * grad
    second_new = beta_second * second + (1.0 - beta_second) * grad * grad
    first_hat = first_new / (1.0 - beta_first**STEP)
    second_hat = second_new / (1.0 - beta_second**STEP)
    weight_new = weight - learn_rate * (
        first_hat / (jnp.sqrt(second_hat) + adam_eps) + weight_decay * weight
    )
    return (grad, weight_new, first_new, second_new)


def swap(piece, axis, distance):
    return lax.ppermute(piece, axis, [(i, i ^ distance) for i in range(lax.axis_size(axis))])


def chip_count():
    return lax.axis_size("ctx") // 2


def after(value, marks):
    return lax.optimization_barrier((value, marks))[0]


def gather_shard(piece, dim):
    got = [swap(piece, "shard", j) for j in range(1, lax.axis_size("shard"))]
    return (jnp.concatenate([piece] + got, axis=dim), got)


def gather_pair(piece, dim):
    return jnp.concatenate([piece, swap(piece, "shard", 1)], axis=dim)


def scatter_pair(terms):
    keep, send = jnp.split(terms, 2, axis=0)
    return keep + swap(send.astype(jnp.bfloat16), "shard", 1).astype(jnp.float32)


def gather_cores(piece, dim):
    return jnp.concatenate([piece, swap(piece, "ctx", 1)], axis=dim)


def tree_sum(terms):
    while len(terms) > 1:
        terms = [terms[i] + terms[i + 1] for i in range(0, len(terms), 2)]
    return terms[0]


def wide_sum(terms):
    return tree_sum([piece.astype(jnp.float32) for piece in terms])


def scatter_cores(terms, dim):
    keep = lax.index_in_dim(terms, 0, dim, keepdims=False)
    send = lax.index_in_dim(terms, 1, dim, keepdims=False)
    return wide_sum([keep, swap(send, "ctx", 1)])


def scatter_chips(terms, dim):
    parts = jnp.split(terms, chip_count(), axis=dim)
    got = [swap(parts[k], "ctx", 2 * k) for k in range(1, len(parts))]
    return (wide_sum([parts[0]] + got), got)


def scatter_shard(terms, dim):
    parts = jnp.split(terms, lax.axis_size("shard"), axis=dim)
    return wide_sum([parts[0]] + [swap(parts[j], "shard", j) for j in range(1, len(parts))])


def gather_rows(piece, begin, end):
    piece = after(piece, begin)
    marks = [swap(piece, "ctx", 2 * k) for k in range(1, chip_count())]
    rows = jnp.concatenate(after([piece] + marks, end), axis=-2)
    split = rows.reshape(rows.shape[:-2] + (chip_count(), 1, piece.shape[-2], rows.shape[-1]))
    whole = gather_cores(split, -3).reshape(
        rows.shape[:-2] + (2 * rows.shape[-2], rows.shape[-1])
    )
    return (whole, marks)


def core_rows(rows):
    split = rows.reshape(rows.shape[:-2] + (chip_count(), 1, -1, rows.shape[-1]))
    return gather_cores(split, -3).reshape(
        rows.shape[:-2] + (2 * rows.shape[-2], rows.shape[-1])
    )


def scatter_rows(terms, begin):
    chips = chip_count()
    rows = terms.shape[-2] // (2 * chips)
    split = terms.reshape(terms.shape[:-2] + (chips, 2, rows, terms.shape[-1]))
    summed = scatter_cores(split, split.ndim - 3).astype(jnp.bfloat16)
    summed = summed.reshape(terms.shape[:-2] + (chips * rows, terms.shape[-1]))
    return scatter_chips(after(summed, begin), -2)


def split_wide(values):
    high = lax.reduce_precision(values, 8, 7)
    low = lax.reduce_precision(values - high, 8, 7)
    return (high + low, jnp.concatenate([high, low], axis=0).astype(jnp.bfloat16))


def join_wide(packed, shape):
    high, low = jnp.split(packed.reshape((2,) + shape).astype(jnp.float32), 2, axis=0)
    return (high + low)[0]


def scatter_last(terms, small, attn_terms):
    chips = chip_count()
    shards_n = lax.axis_size("shard")
    rows = terms.shape[0] // (2 * chips)
    shape = small.shape
    split = terms.reshape(chips, 2, rows, terms.shape[1])
    summed = scatter_cores(split, 1).astype(jnp.bfloat16)
    small = small + swap(small, "ctx", 1)
    own, packed = split_wide(small)
    packed = packed.reshape(-1, terms.shape[1])
    got = [
        swap(jnp.concatenate([summed[k], packed], axis=0), "ctx", 2 * k)
        for k in range(1, chips)
    ]
    small = tree_sum([own] + [join_wide(piece[rows:], shape) for piece in got])
    summed = wide_sum([summed[0]] + [piece[:rows] for piece in got]).astype(jnp.bfloat16)
    own, packed = split_wide(small)
    attn_parts = jnp.split(attn_terms.astype(jnp.bfloat16), shards_n, axis=-1)
    parts = jnp.split(summed, shards_n, axis=1)
    width = attn_parts[0].shape[-1]

    def flat(value):
        return value.reshape(-1, width)

    def message(j):
        return jnp.concatenate([flat(packed), flat(attn_parts[j]), flat(parts[j])], axis=0)

    mine = message(0)
    got = [swap(message(j), "shard", j) for j in range(1, shards_n)]
    small_rows = packed.size // width
    attn_rows = small_rows + attn_parts[0].size // width
    term_rows = attn_rows + parts[0].size // width
    small = tree_sum([own] + [join_wide(piece[:small_rows], shape) for piece in got])
    total = wide_sum([mine[small_rows:term_rows]] + [piece[small_rows:term_rows] for piece in got])
    return (
        total[: attn_rows - small_rows].reshape(attn_parts[0].shape),
        total[attn_rows - small_rows :].reshape(parts[0].shape),
        small,
    )


def relative_ctx(index):
    return lax.axis_index("ctx") ^ index


def one_hot(source):
    size = source.shape[0]
    return (jnp.arange(size, dtype=jnp.int32)[:, None] == source[None, :]).astype(jnp.bfloat16)


def nn(left, right):
    return jnp.dot(left, right, preferred_element_type=jnp.float32)


def nt(left, right):
    return lax.dot_general(
        left, right, (((1,), (1,)), ((), ())), preferred_element_type=jnp.float32
    )


def tn(left, right):
    return lax.dot_general(
        left, right, (((0,), (0,)), ((), ())), preferred_element_type=jnp.float32
    )


def stack_heads(rows, half_len):
    return jnp.concatenate(
        [
            rows[side * half_len : (side + 1) * half_len, h * HEAD : (h + 1) * HEAD]
            for side in range(2)
            for h in range(HEADS)
        ],
        axis=0,
    )


def key_block(kv_ref, table_ref, block_index, shard_size, part):
    half_blocks = table_ref.shape[0] - 2
    high = (block_index >= half_blocks).astype(jnp.int32)
    at = table_ref[jnp.where(high == 1, 2 * half_blocks - 1 - block_index, block_index)]
    piece = kv_ref[at, :, high, :, part * HEAD : (part + 1) * HEAD]
    return piece.reshape(piece.shape[0] * piece.shape[1], HEAD)


def start_keys(piece_refs, kv_ref, sem_ref):
    copies = [
        pltpu.make_async_copy(piece_ref, kv_ref.at[i], sem_ref.at[i])
        for i, piece_ref in enumerate(piece_refs)
    ]
    for copy in copies:
        copy.start()
    return copies


def forward_kernel(table_ref, query_ref, *refs):
    half_blocks = table_ref.shape[0] - 2
    piece_refs = refs[:half_blocks]
    out_ref, log_ref, q_s, acc_s, sum_s, kv_ref, sem_ref = refs[half_blocks:]
    copies = start_keys(piece_refs, kv_ref, sem_ref)
    shard_size = kv_ref.shape[1]
    half_len = kv_ref.shape[3]
    block_len = shard_size * half_len
    side_rows = half_len * HEADS
    own_block = table_ref[half_blocks]
    own_shard = table_ref[half_blocks + 1]
    far_block = 2 * half_blocks - 1 - own_block
    q_s[...] = stack_heads(query_ref[...], half_len)
    acc_s[...] = jnp.zeros_like(acc_s)
    sum_s[...] = jnp.zeros_like(sum_s)
    key_i = lax.broadcasted_iota(jnp.int32, (1, block_len), 1)
    key_in = ((key_i // half_len) ^ own_shard) * half_len + key_i % half_len
    row_i = lax.broadcasted_iota(jnp.int32, (side_rows, 1), 0)
    query_in = own_shard * half_len + row_i % half_len
    offset_in = key_in - query_in
    for copy in copies:
        copy.wait()

    def attend(unit):
        far = (unit > own_block).astype(jnp.int32)
        block_index = unit - far * (own_block + 1)
        query_block = jnp.where(far == 1, far_block, own_block)
        rows = pl.ds(pl.multiple_of(far * side_rows, side_rows), side_rows)
        keys = key_block(kv_ref, table_ref, block_index, shard_size, 0)
        values = key_block(kv_ref, table_ref, block_index, shard_size, 1)
        scores = nt(q_s[rows, :], keys) * score_scale
        visible = offset_in <= (query_block - block_index) * block_len
        weights = jnp.where(visible, jnp.exp(scores), 0.0)
        return (
            rows,
            jnp.sum(weights, axis=-1, keepdims=True),
            nn(weights.astype(jnp.bfloat16), values),
        )

    def attend_some(first, count):
        for rows, total, mixed in [attend(first + i) for i in range(count)]:
            sum_s[rows, :] += total
            acc_s[rows, :] += mixed

    unit_count = 2 * half_blocks + 1
    group = 4

    def attend_group(index, carry):
        attend_some(index * group, group)
        return carry

    lax.fori_loop(0, unit_count // group, attend_group, 0)
    attend_some(unit_count - unit_count % group, unit_count % group)
    total = sum_s[...]
    result = acc_s[...] / total
    log_ref[...] = jnp.log(total)
    for side in range(2):
        for h in range(HEADS):
            at = (side * HEADS + h) * half_len
            out_ref[side * half_len : (side + 1) * half_len, h * HEAD : (h + 1) * HEAD] = result[
                at : at + half_len, :
            ]


def backward_kernel(
    table_ref, query_ref, out_ref, grad_ref, log_ref, *refs
):
    half_blocks = table_ref.shape[0] - 2
    piece_refs = refs[:half_blocks]
    dq_ref, keep_ref, send_ref = refs[half_blocks : half_blocks + 3]
    q_s, do_s, acc_s, log_s, delta_s, kv_ref, dkv_ref, sem_ref = refs[half_blocks + 3 :]
    copies = start_keys(piece_refs, kv_ref, sem_ref)
    shard_size = kv_ref.shape[1]
    half_len = kv_ref.shape[3]
    block_len = shard_size * half_len
    side_rows = half_len * HEADS
    own_block = table_ref[half_blocks]
    own_shard = table_ref[half_blocks + 1]
    far_block = 2 * half_blocks - 1 - own_block
    q_s[...] = stack_heads(query_ref[...], half_len)
    grads = stack_heads(grad_ref[...], half_len)
    do_s[...] = grads
    outs = stack_heads(out_ref[...], half_len)
    delta_all = jnp.transpose(
        jnp.sum(grads.astype(jnp.float32) * outs, axis=-1, keepdims=True)
    )
    log_all = jnp.transpose(log_ref[...])
    acc_s[...] = jnp.zeros_like(acc_s)
    shape = (shard_size, half_len, HEAD)
    for side in range(2):
        log_s[side] = log_all[:, side * side_rows : (side + 1) * side_rows]
        delta_s[side] = delta_all[:, side * side_rows : (side + 1) * side_rows]
    key_i = lax.broadcasted_iota(jnp.int32, (block_len, 1), 0)
    key_in = ((key_i // half_len) ^ own_shard) * half_len + key_i % half_len
    row_i = lax.broadcasted_iota(jnp.int32, (1, side_rows), 1)
    query_in = own_shard * half_len + row_i % half_len
    offset_in = key_in - query_in
    for copy in copies:
        copy.wait()

    def attend(unit):
        far = (unit > own_block).astype(jnp.int32)
        block_index = unit - far * (own_block + 1)
        query_block = jnp.where(far == 1, far_block, own_block)
        rows = pl.ds(pl.multiple_of(far * side_rows, side_rows), side_rows)
        high = (block_index >= half_blocks).astype(jnp.int32)
        at = table_ref[jnp.where(high == 1, 2 * half_blocks - 1 - block_index, block_index)]
        keys = key_block(kv_ref, table_ref, block_index, shard_size, 0)
        values = key_block(kv_ref, table_ref, block_index, shard_size, 1)
        queries = q_s[rows, :]
        grad_rows = do_s[rows, :]
        scores = nt(keys, queries) * score_scale
        visible = offset_in <= (query_block - block_index) * block_len
        weights = jnp.where(visible, jnp.exp(scores - log_s[far]), 0.0)
        grad_weights = nt(values, grad_rows)
        grad_scores = (weights * (grad_weights - delta_s[far])).astype(jnp.bfloat16)
        dq = tn(grad_scores, keys)
        dk = nn(grad_scores, queries) * score_scale
        dv = nn(weights.astype(jnp.bfloat16), grad_rows)
        seen = jnp.logical_and(far == 1, block_index <= own_block)
        return (rows, (at % 2, at // 2), high, seen, dq, dk, dv)

    def attend_some(first, count):
        for rows, (core, chip), high, seen, dq, dk, dv in [attend(first + i) for i in range(count)]:
            acc_s[rows, :] += dq
            for part, value in enumerate((dk, dv)):
                columns = slice(part * HEAD, (part + 1) * HEAD)
                old = dkv_ref[core, chip, :, high, :, columns].astype(jnp.float32)
                dkv_ref[core, chip, :, high, :, columns] = (
                    value.reshape(shape) + jnp.where(seen, old, 0.0)
                ).astype(jnp.bfloat16)

    def none(block_index, carry):
        at = table_ref[2 * half_blocks - 1 - block_index]
        dkv_ref[at % 2, at // 2, :, 1] = jnp.zeros(
            (shard_size, half_len, 2 * HEAD), jnp.bfloat16
        )
        return carry

    unit_count = 2 * half_blocks + 1
    group = 4

    def attend_group(index, carry):
        attend_some(index * group, group)
        return carry

    lax.fori_loop(0, unit_count // group, attend_group, 0)
    attend_some(unit_count - unit_count % group, unit_count % group)
    lax.fori_loop(far_block + 1, 2 * half_blocks, none, 0)
    copies = [
        pltpu.make_async_copy(dkv_ref.at[i], target_ref, sem_ref.at[i])
        for i, target_ref in enumerate((keep_ref, send_ref))
    ]
    for copy in copies:
        copy.start()
    result = acc_s[...] * score_scale
    for side in range(2):
        for h in range(HEADS):
            at = (side * HEADS + h) * half_len
            dq_ref[side * half_len : (side + 1) * half_len, h * HEAD : (h + 1) * HEAD] = result[
                at : at + half_len, :
            ]
    for copy in copies:
        copy.wait()


def whole_spec(space=pltpu.VMEM):
    return pl.BlockSpec(memory_space=space)


def attention_forward(table, queries, pieces):
    rows = queries.shape[0] * HEADS
    kv_size = len(pieces) * pieces[0].size
    return pl.pallas_call(
        forward_kernel,
        out_shape=(
            jax.ShapeDtypeStruct(queries.shape, jnp.float32),
            jax.ShapeDtypeStruct((rows, 1), jnp.float32),
        ),
        in_specs=[whole_spec(pltpu.SMEM), whole_spec()] + [whole_spec(pl.ANY)] * len(pieces),
        out_specs=(whole_spec(), whole_spec()),
        scratch_shapes=[
            pltpu.VMEM((rows, HEAD), jnp.bfloat16),
            pltpu.VMEM((rows, HEAD), jnp.float32),
            pltpu.VMEM((rows, 1), jnp.float32),
            pltpu.VMEM((len(pieces),) + pieces[0].shape, jnp.bfloat16),
            pltpu.SemaphoreType.DMA((len(pieces),)),
        ],
        compiler_params=pltpu.CompilerParams(vmem_limit_bytes=2 * kv_size + (24 << 20)),
        name="attention_forward",
    )(table, queries, *pieces)


def attention_backward(table, queries, pieces, outs, grads, logs):
    rows = queries.shape[0] * HEADS
    kv_size = len(pieces) * pieces[0].size
    half = (len(pieces) // 2,) + pieces[0].shape
    return pl.pallas_call(
        backward_kernel,
        out_shape=(
            jax.ShapeDtypeStruct(queries.shape, jnp.float32),
            jax.ShapeDtypeStruct(half, jnp.bfloat16),
            jax.ShapeDtypeStruct(half, jnp.bfloat16),
        ),
        in_specs=[whole_spec(pltpu.SMEM)]
        + [whole_spec()] * 4
        + [whole_spec(pl.ANY)] * len(pieces),
        out_specs=(whole_spec(), whole_spec(pl.ANY), whole_spec(pl.ANY)),
        scratch_shapes=[
            pltpu.VMEM((rows, HEAD), jnp.bfloat16),
            pltpu.VMEM((rows, HEAD), jnp.bfloat16),
            pltpu.VMEM((rows, HEAD), jnp.float32),
            pltpu.VMEM((2, 1, rows // 2), jnp.float32),
            pltpu.VMEM((2, 1, rows // 2), jnp.float32),
            pltpu.VMEM((len(pieces),) + pieces[0].shape, jnp.bfloat16),
            pltpu.VMEM((2,) + half, jnp.bfloat16),
            pltpu.SemaphoreType.DMA((len(pieces),)),
        ],
        compiler_params=pltpu.CompilerParams(vmem_limit_bytes=4 * kv_size + (24 << 20)),
        name="attention_backward",
    )(table, queries, outs, grads, logs, *pieces)


def shards(
    tokens,
    positions,
    cotangent,
    query_weight,
    query_first,
    query_second,
    keyval_weight,
    keyval_first,
    keyval_second,
    output_weight,
    output_first,
    output_second,
    gateup_weight,
    gateup_first,
    gateup_second,
    down_weight,
    down_first,
    down_second,
    norm_scales,
    norm_first,
    norm_second,
    head_scales,
    head_first,
    head_second,
):
    bfloat = jnp.bfloat16
    single = jnp.float32
    ctx_size = lax.axis_size("ctx")
    shard_size = lax.axis_size("shard")
    ctx_at = lax.axis_index("ctx")
    shard_at = lax.axis_index("shard")
    row_count, width = tokens.shape
    half_len = row_count // 2
    block_len = half_len * shard_size
    piece_len = width // ctx_size
    slice_len = HEAD // shard_size

    group_tokens, token_marks = gather_shard(tokens, 0)
    attn_pieces, _ = gather_shard(
        jnp.concatenate(
            [
                keyval_weight[0].astype(bfloat),
                keyval_weight[1].astype(bfloat),
                query_weight.astype(bfloat),
                output_weight.astype(bfloat).T,
            ],
            axis=-1,
        )[None],
        0,
    )
    ffn_piece = after(
        jnp.stack(
            [
                gateup_weight[0].astype(bfloat),
                gateup_weight[1].astype(bfloat),
                down_weight.astype(bfloat).T,
            ]
        ),
        token_marks,
    )
    ffn_z = jnp.concatenate(
        [ffn_piece] + [swap(ffn_piece, "shard", j) for j in range(2, shard_size, 2)], axis=-1
    )

    def side_by_side(start, size):
        return jnp.concatenate(
            [attn_pieces[j, :, start : start + size] for j in range(shard_size)], axis=-1
        )

    keyval_full, keyval_marks = gather_rows(side_by_side(0, 2 * slice_len), [], [])

    feature = jnp.arange(width, dtype=jnp.int32)
    feature_map = one_hot(relative_ctx(feature // piece_len) * piece_len + feature % piece_len)
    channel = jnp.arange(2 * HEAD, dtype=jnp.int32)
    channel_map = one_hot(
        ((channel % HEAD) // slice_len ^ shard_at) * (2 * slice_len)
        + (channel // HEAD) * slice_len
        + channel % slice_len
    )
    keyval_sorted = nn(keyval_full, channel_map).astype(bfloat)

    scales = lax.dot_general(
        norm_scales,
        feature_map.astype(single),
        (((1,), (0,)), ((), ())),
        precision=lax.Precision.HIGHEST,
        preferred_element_type=single,
    )
    group_inputs = nn(group_tokens, feature_map)
    inputs = group_inputs[:row_count]
    upstream = nn(cotangent, feature_map)

    ctx_places = lax.dynamic_slice_in_dim(
        positions, ctx_at * shard_size * row_count, shard_size * row_count
    ).reshape(shard_size, row_count)
    piece = jnp.arange(shard_size, dtype=jnp.int32)
    group_at = jnp.sum(
        jnp.where(
            ((piece ^ shard_at)[:, None] == piece[None, :])[:, :, None], ctx_places[None], 0
        ),
        axis=1,
    ).reshape(-1)
    first_at = positions.reshape(ctx_size, shard_size * row_count)[:, 0] // block_len
    rel = jnp.arange(ctx_size, dtype=jnp.int32)
    blocks_rel = jnp.sum(
        jnp.where(relative_ctx(rel)[:, None] == rel[None, :], first_at[None, :], 0), axis=1
    )
    places = jnp.sum(
        jnp.where(blocks_rel[None, :] == rel[:, None], rel[None, :], 0), axis=1
    )
    table = jnp.concatenate(
        [places, blocks_rel[:1], jnp.full((1,), shard_at, jnp.int32)]
    ).astype(jnp.int32)

    group_normed, group_inverse = rms_forward(group_inputs)
    group_in = (group_normed * (1.0 + scales[0])).astype(bfloat)
    normed_in, inverse_in = (group_normed[:row_count], group_inverse[:row_count])
    attn_in = group_in[:row_count]
    group_cosine, group_sine = rope_tables(group_at)
    cosine, sine = (group_cosine[:row_count], group_sine[:row_count])
    keyval_proj = nn(group_in, keyval_sorted)
    group_key_normed, group_key_inverse = rms_forward(keyval_proj[:, :HEAD])
    key_normed, key_inverse = (group_key_normed[:row_count], group_key_inverse[:row_count])
    key_scaled = group_key_normed * (1.0 + head_scales[1])
    keys_own = (key_scaled * group_cosine + rotate(key_scaled) * group_sine).astype(bfloat)
    values_own = keyval_proj[:, HEAD:].astype(bfloat)
    kv_own = jnp.concatenate([keys_own, values_own], axis=-1).reshape(
        shard_size, 2, half_len, 2 * HEAD
    )
    attn_own = jnp.stack(
        [side_by_side(2 * slice_len, HEAD), side_by_side(2 * slice_len + HEAD, HEAD)]
    )
    attn_got = [attn_own] + [swap(attn_own, "ctx", 2 * k) for k in range(1, chip_count())]
    kv_marks = [swap(kv_own, "ctx", 2 * k) for k in range(1, chip_count())]
    attn_got = after(attn_got, (kv_marks, ffn_z))
    attn_full = core_rows(jnp.concatenate(attn_got, axis=-2))
    query_full, output_full = (attn_full[0], attn_full[1])
    query_proj = nn(attn_in, query_full)
    query_heads = [
        rms_forward(query_proj[:, h * HEAD : (h + 1) * HEAD]) for h in range(HEADS)
    ]

    def turn(values):
        return values * cosine + rotate(values) * sine

    query_rows = jnp.concatenate(
        [turn(normed * (1.0 + head_scales[0])).astype(bfloat) for normed, _ in query_heads],
        axis=1,
    )
    kv_pieces = [
        piece
        for own in [kv_own] + kv_marks
        for piece in (own, swap(own, "ctx", 1))
    ]

    attn_rows, attn_logs = attention_forward(table, query_rows, kv_pieces)
    ffn_full, _ = gather_rows(ffn_z, kv_marks, attn_rows)
    gate_full, up_full, down_full = (ffn_full[0], ffn_full[1], ffn_full[2])
    attn_b = attn_rows.astype(bfloat)
    attn_out = nt(attn_b, output_full)
    out_normed, out_inverse = rms_forward(attn_out)
    hidden_in = inputs + out_normed * (1.0 + scales[1])
    mid_normed, mid_inverse = rms_forward(hidden_in)
    ffn_in = (mid_normed * (1.0 + scales[2])).astype(bfloat)
    group_ffn = gather_pair(ffn_in, 0)
    gate_pre = nn(group_ffn, gate_full)
    up_pre = nn(group_ffn, up_full)
    gate_value, gate_slope = gelu_parts(gate_pre)
    hidden_b = (gate_value * up_pre).astype(bfloat)
    ffn_out = scatter_pair(nt(hidden_b, down_full))
    ffn_normed, ffn_inverse = rms_forward(ffn_out)
    block_out = nt(
        (hidden_in + ffn_normed * (1.0 + scales[3])).astype(bfloat), feature_map
    ).astype(bfloat)
    grad_norm3 = jnp.sum(upstream * ffn_normed, axis=0)
    ffn_grad = rms_backward(ffn_normed, ffn_inverse, upstream * (1.0 + scales[3])).astype(bfloat)
    group_grad = gather_pair(ffn_grad, 0)
    hidden_grad = nn(group_grad, down_full)
    gate_grad = (hidden_grad * up_pre * gate_slope).astype(bfloat)
    up_grad = (hidden_grad * gate_value).astype(bfloat)
    ffn_in_grad = scatter_pair(nt(gate_grad, gate_full) + nt(up_grad, up_full))
    ffn_rows, ffn_marks = scatter_rows(
        jnp.stack(
            [
                tn(group_ffn, gate_grad).astype(bfloat),
                tn(group_ffn, up_grad).astype(bfloat),
                tn(group_grad, hidden_b).astype(bfloat),
            ]
        ),
        [],
    )
    ffn_parts = jnp.split(ffn_rows.astype(bfloat), shard_size // 2, axis=-1)
    ffn_owned = wide_sum(
        [ffn_parts[0]] + [swap(ffn_parts[j], "shard", 2 * j) for j in range(1, len(ffn_parts))]
    )
    grad_norm2 = jnp.sum(ffn_in_grad * mid_normed, axis=0)
    residual_grad = upstream + rms_backward(mid_normed, mid_inverse, ffn_in_grad * (1.0 + scales[2]))
    grad_norm1 = jnp.sum(residual_grad * out_normed, axis=0)
    attn_out_grad = rms_backward(
        out_normed, out_inverse, residual_grad * (1.0 + scales[1])
    ).astype(bfloat)
    attn_grad_b = nn(attn_out_grad, output_full).astype(bfloat)
    query_parts, kv_keep, kv_send = attention_backward(
        table, query_rows, kv_pieces, attn_rows, attn_grad_b, attn_logs
    )
    kv_keep, kv_send = after((kv_keep, kv_send), ffn_marks)
    kv_terms = wide_sum([kv_keep, swap(kv_send, "ctx", 1)]).astype(bfloat)
    kv_core = kv_terms
    kv_terms, kv_marks = scatter_chips(kv_terms, 0)
    kv_grad = scatter_shard(kv_terms.astype(bfloat)[0], 0).reshape(row_count, 2 * HEAD)
    query_rope_grads = []
    for h in range(HEADS):
        part = query_parts[:, h * HEAD : (h + 1) * HEAD]
        query_rope_grads.append(part * cosine + rotate_back(part * sine))
    grad_head0 = sum(
        jnp.sum(part * normed, axis=0) for part, (normed, _) in zip(query_rope_grads, query_heads)
    )
    query_proj_grad = jnp.concatenate(
        [
            rms_backward(normed, inverse, part * (1.0 + head_scales[0])).astype(bfloat)
            for part, (normed, inverse) in zip(query_rope_grads, query_heads)
        ],
        axis=1,
    )
    late_grad, late_out_grad = after((query_proj_grad, attn_out_grad), kv_core)
    query_wgrad = tn(attn_in, late_grad).astype(bfloat)
    output_wgrad = tn(late_out_grad, attn_b).astype(bfloat)
    attn_terms, attn_marks = scatter_rows(jnp.stack([query_wgrad, output_wgrad]), kv_marks)
    kv_grad = after(kv_grad, attn_marks)
    key_rot_grad = kv_grad[:, :HEAD]
    value_grad = kv_grad[:, HEAD:]
    key_rope_grad = key_rot_grad * cosine + rotate_back(key_rot_grad * sine)
    grad_head1 = jnp.sum(key_rope_grad * key_normed, axis=0)
    key_proj_grad = rms_backward(
        key_normed, key_inverse, key_rope_grad * (1.0 + head_scales[1])
    ).astype(bfloat)
    keyval_proj_grad = jnp.concatenate([key_proj_grad, value_grad.astype(bfloat)], axis=-1)
    keyval_wgrad = nt(tn(attn_in, keyval_proj_grad).astype(bfloat), channel_map).astype(bfloat)
    attn_in_grad = nt(query_proj_grad, query_full) + nt(keyval_proj_grad, keyval_sorted)
    grad_norm0 = jnp.sum(attn_in_grad * normed_in, axis=0)
    tokens_grad = nt(
        (
            residual_grad
            + rms_backward(normed_in, inverse_in, attn_in_grad * (1.0 + scales[0]))
        ).astype(bfloat),
        feature_map,
    ).astype(bfloat)
    norm_terms = lax.dot_general(
        jnp.stack([grad_norm0, grad_norm1, grad_norm2, grad_norm3]),
        feature_map.astype(single),
        (((1,), (1,)), ((), ())),
        precision=lax.Precision.HIGHEST,
        preferred_element_type=single,
    )
    attn_owned, keyval_owned, small = scatter_last(
        keyval_wgrad,
        jnp.concatenate([norm_terms.reshape(-1), grad_head0, grad_head1]).reshape(-1, 128),
        attn_terms,
    )
    small = small.reshape(-1)
    norm_wgrad = small[: 4 * width].reshape(4, width)
    head_wgrad = small[4 * width :].reshape(2, HEAD)

    query_set = adam_update(query_weight, query_first, query_second, attn_owned[0])
    keyval_set = adam_update(
        keyval_weight,
        keyval_first,
        keyval_second,
        jnp.stack([keyval_owned[:, :slice_len], keyval_owned[:, slice_len:]]),
    )
    output_set = adam_update(output_weight, output_first, output_second, attn_owned[1].T)
    gateup_set = adam_update(
        gateup_weight, gateup_first, gateup_second, ffn_owned[:2]
    )
    down_set = adam_update(down_weight, down_first, down_second, ffn_owned[2].T)
    norm_set = adam_update(norm_scales, norm_first, norm_second, norm_wgrad)
    head_set = adam_update(head_scales, head_first, head_second, head_wgrad)
    return (
        (block_out, tokens_grad)
        + query_set
        + keyval_set
        + output_set
        + gateup_set
        + down_set
        + norm_set
        + head_set
    )


def solution(mesh):
    placed = (
        P(("ctx", "shard"), None),
        P(),
        P(("ctx", "shard"), None),
        P("ctx", "shard"),
        P("ctx", "shard"),
        P("ctx", "shard"),
        P(None, "ctx", "shard"),
        P(None, "ctx", "shard"),
        P(None, "ctx", "shard"),
        P("shard", "ctx"),
        P("shard", "ctx"),
        P("shard", "ctx"),
        P(None, "ctx", "shard"),
        P(None, "ctx", "shard"),
        P(None, "ctx", "shard"),
        P("shard", "ctx"),
        P("shard", "ctx"),
        P("shard", "ctx"),
        P(),
        P(),
        P(),
        P(),
        P(),
        P(),
    )
    return jax.shard_map(
        shards,
        mesh=mesh,
        in_specs=placed,
        out_specs=(
            P(("ctx", "shard"), None),
            P(("ctx", "shard"), None),
            P("ctx", "shard"),
            P("ctx", "shard"),
            P("ctx", "shard"),
            P("ctx", "shard"),
            P(None, "ctx", "shard"),
            P(None, "ctx", "shard"),
            P(None, "ctx", "shard"),
            P(None, "ctx", "shard"),
            P("shard", "ctx"),
            P("shard", "ctx"),
            P("shard", "ctx"),
            P("shard", "ctx"),
            P(None, "ctx", "shard"),
            P(None, "ctx", "shard"),
            P(None, "ctx", "shard"),
            P(None, "ctx", "shard"),
            P("shard", "ctx"),
            P("shard", "ctx"),
            P("shard", "ctx"),
            P("shard", "ctx"),
            P(),
            P(),
            P(),
            P(),
            P(),
            P(),
            P(),
            P(),
        ),
        check_vma=False,
    )
```
